128 devices in a mesh: row: 8 (over z, core), col: 16 (over y, x).
Axes of the slice: x: 4, y: 4, z: 4, core: 2. Of those that a mesh axis runs over, the one named last changes fastest.
Arguments:
- points: float32 [524288, 64], P(('row', 'col')), may hold values from -6 to 6
- factor: float32 [524288, 512], P(('row', 'col')), may hold values from -0.06 to 0.06
- pivots: int32 [2, 128], replicated, may hold values from 0 to 524287, as said below
Outputs:
- factor_new: float32 [524288, 256], P(('row', 'col'))
- gram_rows: float32 [256, 768], replicated
The draws below stay inside these ranges and needn't reach their ends.
Inputs may be any that keep to these rules, and one draw needn't show every extreme that they name: All 256 pivots are different points.
All inputs are finite; a program needn't handle non-finite values.
Results may differ from the reference program's by a relative error of at most 0.00013.
Values sent between devices are 32-bit elements; how exact they have to be, the bound alone decides.
A program may use at most 128 MiB of HBM per device.

```python
import jax
import jax.numpy as jnp
from jax import lax

DIM = 64
RANK = 512
BLOCK = 128
BLOCKS = 2
PTS_DEV = 4096
NPTS = 524288


def draw_pivots(key, part):
    chosen = jax.random.choice(key, NPTS, (BLOCKS * BLOCK,), replace=False)
    return chosen.reshape(BLOCKS, BLOCK).astype(jnp.int32)


def shard_levels(key, shape, shards, smallest, largest):
    gain = 1.0
    for position, shards_of in shards:
        heights = jax.random.uniform(jax.random.fold_in(jax.random.fold_in(key, 6), position), (shards_of,), jnp.float32, smallest / len(shards), largest / len(shards))
        gain = gain * jnp.repeat(jnp.exp(heights), shape[position] // shards_of).reshape((-1,) + (1,) * (len(shape) - 1 - position))
    return gain


def normal_values(rng, dims, deviation, bound, split=(), held_as=jnp.bfloat16):
    drawn = deviation * jax.random.normal(rng, dims, jnp.float32)
    if split:
        drawn = drawn * shard_levels(rng, dims, split, -0.22, 0.18)
    return jnp.clip(drawn, -bound, bound).astype(held_as)


def setup_inputs(seed: int = 0) -> dict:
    keys = jax.random.split(jax.random.key(seed), 4)
    return {
        "points": normal_values(keys[0], (NPTS, DIM), 1.0, 6.0, ((0, 128),), jnp.float32),
        "factor": normal_values(keys[1], (NPTS, RANK), 0.01, 0.06, ((0, 128),), jnp.float32),
        "pivots": draw_pivots(jax.random.fold_in(keys[3], 71), 0),
    }


highest = lax.Precision.HIGHEST
nugget = 0.1

def kernel_block(left, right):
    cross = jnp.dot(left, right.T, precision=highest)
    dist = jnp.sum(left * left, 1)[:, None] + jnp.sum(right * right, 1)[None, :] - 2.0 * cross
    return jnp.exp(-dist / left.shape[1])

def pivot_inverse(pivot_points, pivot_factor):
    size = pivot_points.shape[0]
    identity = jnp.eye(size, dtype=jnp.float32)
    outer = jnp.dot(pivot_factor, pivot_factor.T, precision=highest)
    shift = nugget + jnp.max(jnp.sum(jnp.abs(outer), 1))
    core = kernel_block(pivot_points, pivot_points) - outer + shift * identity
    lower = jnp.linalg.cholesky(core)
    return jax.scipy.linalg.solve_triangular(lower, identity, lower=True)

def new_columns(rows_points, rows_factor, pivot_points, pivot_factor, inverse):
    resid = kernel_block(rows_points, pivot_points) - jnp.dot(rows_factor, pivot_factor.T, precision=highest)
    return jnp.dot(resid, inverse.T, precision=highest)

def reference(points, factor, pivots):
    current = factor
    made = []
    for section in range(BLOCKS):
        indices = pivots[section].astype(jnp.int32)
        pivot_points = points[indices]
        pivot_factor = current[indices]
        inverse = pivot_inverse(pivot_points, pivot_factor)
        fresh = new_columns(points, current, pivot_points, pivot_factor, inverse)
        made.append(fresh)
        current = jnp.concatenate([current, fresh], 1)
    factor_new = jnp.concatenate(made, 1)
    gram_rows = jnp.dot(factor_new.T, current, precision=highest) / PTS_DEV
    return (factor_new, gram_rows)
```

```python
import functools

import jax
import jax.numpy as jnp
from jax import lax
from jax.experimental import pallas as pl
from jax.experimental.pallas import tpu as pltpu
from jax.sharding import PartitionSpec as P

f32 = jnp.float32
bf16 = jnp.bfloat16
MESH = pl.DeviceIdType.MESH
CHIPS = 64
NUGGET = 0.1
MB = 1 << 20

NT = (((1,), (1,)), ((), ()))
TN = (((0,), (0,)), ((), ()))
NN = (((1,), (0,)), ((), ()))


def exact(a, b, dims=NN):
    return lax.dot_general(a, b, dims, precision=lax.Precision.HIGHEST, preferred_element_type=f32)


def mm(a, b, dims=NN):
    return lax.dot_general(a, b, dims, preferred_element_type=f32)


def halves(a):
    high = a.astype(bf16)
    return high, (a - high.astype(f32)).astype(bf16)


def offsets():
    def hops(d):
        return sum(min(c, 4 - c) for c in (d // 16, d // 4 % 4, d % 4))

    return sorted(range(1, CHIPS), key=lambda d: (-hops(d), d))


class Place:
    def __init__(self):
        row, col = lax.axis_index("row"), lax.axis_index("col")
        self.core, z = row % 2, row // 2
        y, x = col // 4, col % 4
        self.chip = z * 16 + col
        self.number = row * 16 + col
        self.other = (row + 1 - 2 * self.core, col)
        zs = [(z + i) % 4 for i in range(4)]
        ys = [(y + i) % 4 for i in range(4)]
        xs = [(x + i) % 4 for i in range(4)]
        self.peers = []
        for d in offsets():
            pz, pc = zs[d // 16], ys[d // 4 % 4] * 4 + xs[d % 4]
            self.peers.append(((pz * 2 + self.core, pc), pz * 16 + pc))


def greet(place):
    barrier = pltpu.get_barrier_semaphore()
    for device, _ in place.peers:
        pl.semaphore_signal(barrier, inc=1, device_id=device, device_id_type=MESH)
    pl.semaphore_signal(barrier, inc=1, device_id=place.other, device_id_type=MESH)


def greeted():
    pl.semaphore_wait(pltpu.get_barrier_semaphore(), CHIPS)


def remote(src, dst, send, recv, device):
    return pltpu.make_async_remote_copy(src, dst, send, recv, device_id=device, device_id_type=MESH)


def device_sum(place, mine, pair, arrived, own, total, send, recv):
    core, chip, other = place.core, place.chip, place.other
    swap = remote(mine.at[1 - core], pair, send.at[0], recv.at[0], other)
    swap.start()
    swap.wait_recv()
    pair[...] = mine[core] + pair[...]
    for slot, (device, target) in enumerate(place.peers):
        remote(pair.at[target], arrived.at[slot], send.at[1], recv.at[1], device).start()
    remote(arrived, arrived, send.at[1], recv.at[1], other).wait_recv()
    own[...] = pair[chip] + jnp.sum(arrived[...], axis=0)
    for device, _ in place.peers:
        remote(own, total.at[core, chip], send.at[2], recv.at[2], device).start()
    total[core, chip] = own[...]
    remote(arrived, arrived, send.at[2], recv.at[2], other).wait_recv()
    back = remote(total.at[core], total.at[core], send.at[3], recv.at[3], other)
    back.start()
    swap.wait_send()
    remote(arrived, arrived, send.at[1], recv.at[1], other).wait_send()
    remote(arrived, arrived, send.at[2], recv.at[2], other).wait_send()
    back.wait()


def sum_scratch(rows):
    return [
        pltpu.VMEM((2, CHIPS, rows, 128), f32),
        pltpu.VMEM((CHIPS, rows, 128), f32),
        pltpu.VMEM((CHIPS - 1, rows, 128), f32),
        pltpu.VMEM((rows, 128), f32),
        pltpu.VMEM((2, CHIPS, rows, 128), f32),
        pltpu.SemaphoreType.DMA((4,)),
        pltpu.SemaphoreType.DMA((4,)),
    ]


def fetch_kernel(pivots, points_hbm, factor_hbm, q_ref, p_ref, points, factor, load, mine, *rest):
    place = Place()
    greet(place)
    loads = [
        pltpu.make_async_copy(points_hbm, points, load.at[0]),
        pltpu.make_async_copy(factor_hbm, factor, load.at[1]),
    ]
    for copy in loads:
        copy.start()
    count, width = points.shape
    first = place.number * count
    for copy in loads:
        copy.wait()

    def pick(i, carry):
        rows = []
        for s in range(2):
            local = pivots[s, i] - first
            inside = ((local >= 0) & (local < count)).astype(jnp.int32).astype(f32)
            local = jnp.clip(local, 0, count - 1)
            rows.append((points[pl.ds(local, 1), :] * inside, factor[pl.ds(local, 1), :] * inside))
        half, chip = i // CHIPS, i % CHIPS
        for s in range(2):
            for j in range(4):
                mine[half, chip, pl.ds(4 * s + j, 1), :] = rows[s][1][:, 128 * j : 128 * (j + 1)]
        mine[half, chip, pl.ds(8, 1), :] = jnp.concatenate([rows[0][0], rows[1][0]], axis=1)
        return carry

    lax.fori_loop(0, 2 * CHIPS, pick, 0, unroll=4)
    greeted()
    total = rest[3]
    device_sum(place, mine, *rest)
    for half in range(2):
        for s in range(2):
            for j in range(4):
                q_ref[pl.ds(128 * s + CHIPS * half, CHIPS), pl.ds(128 * j, 128)] = total[half, :, 4 * s + j, :]
        p_ref[pl.ds(CHIPS * half, CHIPS), :] = total[half, :, 8, :]


def fetch(points, factor, pivots):
    return pl.pallas_call(
        fetch_kernel,
        out_shape=(jax.ShapeDtypeStruct((256, 512), f32), jax.ShapeDtypeStruct((128, 128), f32)),
        in_specs=[
            pl.BlockSpec(memory_space=pltpu.SMEM),
            pl.BlockSpec(memory_space=pl.ANY),
            pl.BlockSpec(memory_space=pl.ANY),
        ],
        out_specs=(pl.BlockSpec(memory_space=pltpu.VMEM), pl.BlockSpec(memory_space=pltpu.VMEM)),
        scratch_shapes=[
            pltpu.VMEM(points.shape, f32),
            pltpu.VMEM(factor.shape, f32),
            pltpu.SemaphoreType.DMA((2,)),
            *sum_scratch(9),
        ],
        compiler_params=pltpu.CompilerParams(collective_id=0, has_side_effects=True, vmem_limit_bytes=40 * MB),
    )(pivots, points, factor)


def residual_kernel(points, factor, q_ref, p_ref, r_ref, m_ref, qh, ql, pt, pn, cross):
    step = pl.program_id(0)
    width = points.shape[1]

    @pl.when(step == 0)
    def _():
        q = q_ref[...].T
        qh[...], ql[...] = halves(q)
        pp = p_ref[...].T
        p = jnp.concatenate([pp[:width], pp[width:]], axis=1) * (2.0 / width)
        high, low = halves(p)
        pt[...] = jnp.concatenate([high, low, high, low], axis=0)
        pn[...] = jnp.sum(p * p, axis=0, keepdims=True) * (width / 4.0)
        m_ref[...] = jnp.zeros_like(m_ref)
        cross[...] = jnp.zeros_like(cross)

    a = points[...]
    high, low = halves(a)
    inner = mm(jnp.concatenate([high, high, low, low], axis=1), pt[...])
    norm = jnp.sum(a * a, axis=1, keepdims=True) * (1.0 / width)
    kernel = jnp.exp(inner - norm - pn[...])
    xh, xl = halves(factor[...])
    r = kernel - (mm(xh, qh[...]) + mm(xh, ql[...]) + mm(xl, qh[...]))
    r_ref[...] = r
    rh, rl = halves(r)
    wide = factor.shape[1]
    m_ref[:, :wide] += mm(rh, xh, TN) + mm(rh, xl, TN) + mm(rl, xh, TN)
    m_ref[:, wide:] += mm(rh, rh, TN)
    cross[...] += mm(rh, rl, TN)

    @pl.when(step == pl.num_programs(0) - 1)
    def _():
        m_ref[:, wide:] += cross[...] + cross[...].T


def residual(points, factor, q, p, tile=256):
    count, width = points.shape
    wide = factor.shape[1]
    size = q.shape[0]
    return pl.pallas_call(
        residual_kernel,
        out_shape=(jax.ShapeDtypeStruct((count, size), f32), jax.ShapeDtypeStruct((size, wide + size), f32)),
        grid=(count // tile,),
        in_specs=[
            pl.BlockSpec((tile, width), lambda i: (i, 0)),
            pl.BlockSpec((tile, wide), lambda i: (i, 0)),
            pl.BlockSpec(q.shape, lambda i: (0, 0)),
            pl.BlockSpec(p.shape, lambda i: (0, 0)),
        ],
        out_specs=(
            pl.BlockSpec((tile, size), lambda i: (i, 0)),
            pl.BlockSpec((size, wide + size), lambda i: (0, 0)),
        ),
        scratch_shapes=[
            pltpu.VMEM((wide, size), bf16),
            pltpu.VMEM((wide, size), bf16),
            pltpu.VMEM((4 * width, size), bf16),
            pltpu.VMEM((1, size), f32),
            pltpu.VMEM((size, size), f32),
        ],
        compiler_params=pltpu.CompilerParams(vmem_limit_bytes=40 * MB),
    )(points, factor, q, p)


def inverse_lower(core, a_ref, t_ref):
    size = core.shape[0]
    rows = lax.broadcasted_iota(jnp.int32, (size, size), 0)
    cols = lax.broadcasted_iota(jnp.int32, (size, size), 1)
    a_ref[...] = core
    t_ref[...] = (rows == cols).astype(f32)
    row = lax.broadcasted_iota(jnp.int32, (size, 1), 0)

    def step(b, carry):
        first = b * 8
        for i in range(8):
            at = first + i
            line = a_ref[pl.ds(at, 1), :]
            made = t_ref[pl.ds(at, 1), :]
            pivot = line[:, i : i + 1]
            scale = jnp.where(row > at, a_ref[:, i : i + 1] * (1.0 / pivot), 0.0)
            scale = jnp.where(row == at, 1.0 - lax.rsqrt(pivot), scale)
            a_ref[...] = a_ref[...] - scale * line
            t_ref[...] = t_ref[...] - scale * made
        a_ref[...] = pltpu.roll(a_ref[...], size - 8, 1)
        return carry

    lax.fori_loop(0, size // 8, step, 0)
    return t_ref[...]


def weights_kernel(q_ref, p_ref, w_ref, a_ref, t_ref):
    q = q_ref[...]
    pp = p_ref[...]
    size, width = pp.shape[0], pp.shape[1] // 2
    p = jnp.concatenate([pp[:, :width], pp[:, width:]], axis=0)
    norm = jnp.sum(p * p, axis=1, keepdims=True)
    across = exact(jnp.ones((8, width), f32), p * p, NT)[:1]
    kernel = jnp.exp((2.0 * exact(p, p, NT) - norm - across) * (1.0 / width))
    outer = exact(q, q, NT)
    rows = lax.broadcasted_iota(jnp.int32, (size, size), 0)
    cols = lax.broadcasted_iota(jnp.int32, (size, size), 1)
    eye = (rows == cols).astype(f32)

    def core(k, g):
        shift = NUGGET + jnp.max(jnp.sum(jnp.abs(g), axis=1, keepdims=True), axis=0, keepdims=True)
        return k - g + shift * eye

    t0 = inverse_lower(core(kernel[:size, :size], outer[:size, :size]), a_ref, t_ref)
    c10 = exact(kernel[size:, :size] - outer[size:, :size], t0, NT)
    g1 = outer[size:, size:] + exact(c10, c10, NT)
    t1 = inverse_lower(core(kernel[size:, size:], g1), a_ref, t_ref)
    t10 = -exact(exact(t1, c10), t0)
    w_ref[:size, :size] = t0.T
    w_ref[:size, size:] = t10.T
    w_ref[size:, :size] = jnp.zeros((size, size), f32)
    w_ref[size:, size:] = t1.T


def weights(q, p):
    size = q.shape[0]
    return pl.pallas_call(
        weights_kernel,
        out_shape=jax.ShapeDtypeStruct((size, size), f32),
        in_specs=[pl.BlockSpec(memory_space=pltpu.VMEM)] * 2,
        out_specs=pl.BlockSpec(memory_space=pltpu.VMEM),
        scratch_shapes=[pltpu.VMEM((size // 2, size // 2), f32)] * 2,
        compiler_params=pltpu.CompilerParams(vmem_limit_bytes=40 * MB),
    )(q, p)


def total_kernel(m_ref, o_ref, mine, *rest):
    place = Place()
    greet(place)
    for k in range(2):
        for h in range(2):
            for j in range(6):
                mine[k, :, 2 * j + h, :] = m_ref[pl.ds(128 * k + CHIPS * h, CHIPS), pl.ds(128 * j, 128)]
    greeted()
    total = rest[3]
    device_sum(place, mine, *rest)
    for k in range(2):
        for h in range(2):
            for j in range(6):
                o_ref[pl.ds(128 * k + CHIPS * h, CHIPS), pl.ds(128 * j, 128)] = total[k, :, 2 * j + h, :]


def total_products(m):
    return pl.pallas_call(
        total_kernel,
        out_shape=jax.ShapeDtypeStruct(m.shape, f32),
        in_specs=[pl.BlockSpec(memory_space=pltpu.VMEM)],
        out_specs=pl.BlockSpec(memory_space=pltpu.VMEM),
        scratch_shapes=sum_scratch(12),
        compiler_params=pltpu.CompilerParams(collective_id=1, has_side_effects=True, vmem_limit_bytes=40 * MB),
    )(m)


def columns_kernel(r_ref, w_ref, m_ref, c_ref, g_ref, wh, wl, *, scale):
    @pl.when(pl.program_id(0) == 0)
    def _():
        w = w_ref[...]
        wh[...], wl[...] = halves(w)
        size = w.shape[0]
        wide = m_ref.shape[1] - size
        turned = w.T
        g_ref[:, :wide] = exact(turned, m_ref[:, :wide]) * scale
        g_ref[:, wide:] = exact(turned, exact(m_ref[:, wide:], w)) * scale

    rh, rl = halves(r_ref[...])
    c_ref[...] = mm(rh, wh[...]) + mm(rh, wl[...]) + mm(rl, wh[...])


def columns(r, w, m, tile=512):
    count, size = r.shape
    return pl.pallas_call(
        functools.partial(columns_kernel, scale=1.0 / count),
        out_shape=(jax.ShapeDtypeStruct(r.shape, f32), jax.ShapeDtypeStruct(m.shape, f32)),
        grid=(count // tile,),
        in_specs=[
            pl.BlockSpec((tile, size), lambda i: (i, 0)),
            pl.BlockSpec(w.shape, lambda i: (0, 0)),
            pl.BlockSpec(m.shape, lambda i: (0, 0)),
        ],
        out_specs=(pl.BlockSpec((tile, size), lambda i: (i, 0)), pl.BlockSpec(m.shape, lambda i: (0, 0))),
        scratch_shapes=[pltpu.VMEM(w.shape, bf16)] * 2,
        compiler_params=pltpu.CompilerParams(vmem_limit_bytes=40 * MB),
    )(r, w, m)


def body(points, factor, pivots):
    q, p = fetch(points, factor, pivots)
    r, m = residual(points, factor, q, p)
    w = weights(q, p)
    m = total_products(m)
    return columns(r, w, m)


def solution(mesh):
    split = P(("row", "col"), None)
    return jax.shard_map(
        body,
        mesh=mesh,
        in_specs=(split, split, P()),
        out_specs=(split, P()),
        check_vma=False,
    )
```

```python
import functools

import jax
import jax.numpy as jnp
from jax import lax
from jax.experimental import pallas as pl
from jax.experimental.pallas import tpu as pltpu
from jax.sharding import PartitionSpec as P

f32 = jnp.float32
bf16 = jnp.bfloat16
MESH = pl.DeviceIdType.MESH
CHIPS = 64
NUGGET = 0.1
MB = 1 << 20

NT = (((1,), (1,)), ((), ()))
TN = (((0,), (0,)), ((), ()))
NN = (((1,), (0,)), ((), ()))


def exact(a, b, dims=NN):
    return lax.dot_general(a, b, dims, precision=lax.Precision.HIGHEST, preferred_element_type=f32)


def mm(a, b, dims=NN):
    return lax.dot_general(a, b, dims, preferred_element_type=f32)


def halves(a):
    high = a.astype(bf16)
    return high, (a - high.astype(f32)).astype(bf16)


def offsets():
    def hops(d):
        return sum(min(c, 4 - c) for c in (d // 16, d // 4 % 4, d % 4))

    return sorted(range(1, CHIPS), key=lambda d: (-hops(d), d))


class Place:
    def __init__(self):
        row, col = lax.axis_index("row"), lax.axis_index("col")
        self.core, z = row % 2, row // 2
        y, x = col // 4, col % 4
        self.chip = z * 16 + col
        self.number = row * 16 + col
        self.other = (row + 1 - 2 * self.core, col)
        zs = [(z + i) % 4 for i in range(4)]
        ys = [(y + i) % 4 for i in range(4)]
        xs = [(x + i) % 4 for i in range(4)]
        self.peers = []
        for d in offsets():
            pz, pc = zs[d // 16], ys[d // 4 % 4] * 4 + xs[d % 4]
            self.peers.append(((pz * 2 + self.core, pc), pz * 16 + pc))


def greet(place):
    barrier = pltpu.get_barrier_semaphore()
    for device, _ in place.peers:
        pl.semaphore_signal(barrier, inc=1, device_id=device, device_id_type=MESH)
    pl.semaphore_signal(barrier, inc=1, device_id=place.other, device_id_type=MESH)


def greeted():
    pl.semaphore_wait(pltpu.get_barrier_semaphore(), CHIPS)


def remote(src, dst, send, recv, device):
    return pltpu.make_async_remote_copy(src, dst, send, recv, device_id=device, device_id_type=MESH)


def device_sum(place, mine, pair, arrived, own, total, send, recv, first=None, second=None):
    core, chip, other = place.core, place.chip, place.other
    swap = remote(mine.at[1 - core], pair, send.at[0], recv.at[0], other)
    swap.start()
    swap.wait_recv()
    pair[...] = mine[core] + pair[...]
    for slot, (device, target) in enumerate(place.peers):
        remote(pair.at[target], arrived.at[slot], send.at[1], recv.at[1], device).start()
    if first is not None:
        first()
    remote(arrived, arrived, send.at[1], recv.at[1], other).wait_recv()
    own[...] = pair[chip] + jnp.sum(arrived[...], axis=0)
    for device, _ in place.peers:
        remote(own, total.at[core, chip], send.at[2], recv.at[2], device).start()
    total[core, chip] = own[...]
    if second is not None:
        second()
    remote(arrived, arrived, send.at[2], recv.at[2], other).wait_recv()
    back = remote(total.at[core], total.at[core], send.at[3], recv.at[3], other)
    back.start()
    swap.wait_send()
    remote(arrived, arrived, send.at[1], recv.at[1], other).wait_send()
    remote(arrived, arrived, send.at[2], recv.at[2], other).wait_send()
    back.wait()


def sum_scratch(rows):
    return [
        pltpu.VMEM((2, CHIPS, rows, 128), f32),
        pltpu.VMEM((CHIPS, rows, 128), f32),
        pltpu.VMEM((CHIPS - 1, rows, 128), f32),
        pltpu.VMEM((rows, 128), f32),
        pltpu.VMEM((2, CHIPS, rows, 128), f32),
        pltpu.SemaphoreType.DMA((4,)),
        pltpu.SemaphoreType.DMA((4,)),
    ]


def fetch_kernel(pivots, points_hbm, factor_hbm, q_ref, p_ref, points, factor, load, mine, *rest):
    place = Place()
    greet(place)
    loads = [
        pltpu.make_async_copy(points_hbm, points, load.at[0]),
        pltpu.make_async_copy(factor_hbm, factor, load.at[1]),
    ]
    for copy in loads:
        copy.start()
    count, width = points.shape
    first = place.number * count
    for copy in loads:
        copy.wait()

    def pick(i, carry):
        rows = []
        for s in range(2):
            local = pivots[s, i] - first
            inside = ((local >= 0) & (local < count)).astype(jnp.int32).astype(f32)
            local = jnp.clip(local, 0, count - 1)
            rows.append((points[pl.ds(local, 1), :] * inside, factor[pl.ds(local, 1), :] * inside))
        half, chip = i // CHIPS, i % CHIPS
        for s in range(2):
            for j in range(4):
                mine[half, chip, pl.ds(4 * s + j, 1), :] = rows[s][1][:, 128 * j : 128 * (j + 1)]
        mine[half, chip, pl.ds(8, 1), :] = jnp.concatenate([rows[0][0], rows[1][0]], axis=1)
        return carry

    lax.fori_loop(0, 2 * CHIPS, pick, 0, unroll=4)
    greeted()
    total = rest[3]
    device_sum(place, mine, *rest)
    for half in range(2):
        for s in range(2):
            for j in range(4):
                q_ref[pl.ds(128 * s + CHIPS * half, CHIPS), pl.ds(128 * j, 128)] = total[half, :, 4 * s + j, :]
        p_ref[pl.ds(CHIPS * half, CHIPS), :] = total[half, :, 8, :]


def fetch(points, factor, pivots):
    return pl.pallas_call(
        fetch_kernel,
        out_shape=(jax.ShapeDtypeStruct((256, 512), f32), jax.ShapeDtypeStruct((128, 128), f32)),
        in_specs=[
            pl.BlockSpec(memory_space=pltpu.SMEM),
            pl.BlockSpec(memory_space=pl.ANY),
            pl.BlockSpec(memory_space=pl.ANY),
        ],
        out_specs=(pl.BlockSpec(memory_space=pltpu.VMEM), pl.BlockSpec(memory_space=pltpu.VMEM)),
        scratch_shapes=[
            pltpu.VMEM(points.shape, f32),
            pltpu.VMEM(factor.shape, f32),
            pltpu.SemaphoreType.DMA((2,)),
            *sum_scratch(9),
        ],
        compiler_params=pltpu.CompilerParams(collective_id=0, has_side_effects=True, vmem_limit_bytes=40 * MB),
    )(pivots, points, factor)


def residual_kernel(points, factor, q_ref, p_ref, r_ref, m_ref, qh, ql, pt, pn, cross):
    step = pl.program_id(0)
    width = points.shape[1]

    @pl.when(step == 0)
    def _():
        q = q_ref[...].T
        qh[...], ql[...] = halves(q)
        pp = p_ref[...].T
        p = jnp.concatenate([pp[:width], pp[width:]], axis=1) * (2.0 / width)
        high, low = halves(p)
        pt[...] = jnp.concatenate([high, low, high, low], axis=0)
        pn[...] = jnp.sum(p * p, axis=0, keepdims=True) * (width / 4.0)
        m_ref[...] = jnp.zeros_like(m_ref)
        cross[...] = jnp.zeros_like(cross)

    a = points[...]
    high, low = halves(a)
    inner = mm(jnp.concatenate([high, high, low, low], axis=1), pt[...])
    norm = jnp.sum(a * a, axis=1, keepdims=True) * (1.0 / width)
    kernel = jnp.exp(inner - norm - pn[...])
    xh, xl = halves(factor[...])
    r = kernel - (mm(xh, qh[...]) + mm(xh, ql[...]) + mm(xl, qh[...]))
    r_ref[...] = r
    rh, rl = halves(r)
    wide = factor.shape[1]
    m_ref[:, :wide] += mm(rh, xh, TN) + mm(rh, xl, TN) + mm(rl, xh, TN)
    m_ref[:, wide:] += mm(rh, rh, TN)
    cross[...] += mm(rh, rl, TN)

    @pl.when(step == pl.num_programs(0) - 1)
    def _():
        m_ref[:, wide:] += cross[...] + cross[...].T


def residual(points, factor, q, p, tile=256):
    count, width = points.shape
    wide = factor.shape[1]
    size = q.shape[0]
    return pl.pallas_call(
        residual_kernel,
        out_shape=(jax.ShapeDtypeStruct((count, size), f32), jax.ShapeDtypeStruct((size, wide + size), f32)),
        grid=(count // tile,),
        in_specs=[
            pl.BlockSpec((tile, width), lambda i: (i, 0)),
            pl.BlockSpec((tile, wide), lambda i: (i, 0)),
            pl.BlockSpec(q.shape, lambda i: (0, 0)),
            pl.BlockSpec(p.shape, lambda i: (0, 0)),
        ],
        out_specs=(
            pl.BlockSpec((tile, size), lambda i: (i, 0)),
            pl.BlockSpec((size, wide + size), lambda i: (0, 0)),
        ),
        scratch_shapes=[
            pltpu.VMEM((wide, size), bf16),
            pltpu.VMEM((wide, size), bf16),
            pltpu.VMEM((4 * width, size), bf16),
            pltpu.VMEM((1, size), f32),
            pltpu.VMEM((size, size), f32),
        ],
        compiler_params=pltpu.CompilerParams(vmem_limit_bytes=40 * MB),
    )(points, factor, q, p)


def inverse_lower(core, a_ref, t_ref):
    size = core.shape[0]
    rows = lax.broadcasted_iota(jnp.int32, (size, size), 0)
    cols = lax.broadcasted_iota(jnp.int32, (size, size), 1)
    a_ref[...] = core
    t_ref[...] = (rows == cols).astype(f32)
    row = lax.broadcasted_iota(jnp.int32, (size, 1), 0)

    def step(b, carry):
        first = b * 8
        for i in range(8):
            at = first + i
            line = a_ref[pl.ds(at, 1), :]
            made = t_ref[pl.ds(at, 1), :]
            pivot = line[:, i : i + 1]
            scale = jnp.where(row > at, a_ref[:, i : i + 1] * (1.0 / pivot), 0.0)
            scale = jnp.where(row == at, 1.0 - lax.rsqrt(pivot), scale)
            a_ref[...] = a_ref[...] - scale * line
            t_ref[...] = t_ref[...] - scale * made
        a_ref[...] = pltpu.roll(a_ref[...], size - 8, 1)
        return carry

    lax.fori_loop(0, size // 8, step, 0)
    return t_ref[...]


def pivot_terms(q_ref, p_ref, core_ref):
    q = q_ref[...]
    pp = p_ref[...]
    width = pp.shape[1] // 2
    p = jnp.concatenate([pp[:, :width], pp[:, width:]], axis=0)
    norm = jnp.sum(p * p, axis=1, keepdims=True)
    across = exact(jnp.ones((8, width), f32), p * p, NT)[:1]
    core_ref[0] = jnp.exp((2.0 * exact(p, p, NT) - norm - across) * (1.0 / width))
    core_ref[1] = exact(q, q, NT)


def shifted(k, g):
    rows = lax.broadcasted_iota(jnp.int32, g.shape, 0)
    cols = lax.broadcasted_iota(jnp.int32, g.shape, 1)
    shift = NUGGET + jnp.max(jnp.sum(jnp.abs(g), axis=1, keepdims=True), axis=0, keepdims=True)
    return k - g + shift * (rows == cols).astype(f32)


def total_kernel(m_ref, q_ref, p_ref, o_ref, w_ref, core_ref, a_ref, t_ref, mine, *rest):
    place = Place()
    greet(place)
    for k in range(2):
        for h in range(2):
            for j in range(6):
                mine[k, :, 2 * j + h, :] = m_ref[pl.ds(128 * k + CHIPS * h, CHIPS), pl.ds(128 * j, 128)]
    greeted()
    total = rest[3]
    size = a_ref.shape[0]

    def first():
        pivot_terms(q_ref, p_ref, core_ref)
        t0 = inverse_lower(shifted(core_ref[0, :size, :size], core_ref[1, :size, :size]), a_ref, t_ref)
        w_ref[:size, :size] = t0.T
        w_ref[size:, :size] = jnp.zeros((size, size), f32)

    def second():
        turned = w_ref[:size, :size]
        c10 = exact(core_ref[0, size:, :size] - core_ref[1, size:, :size], turned)
        g1 = core_ref[1, size:, size:] + exact(c10, c10, NT)
        t1 = inverse_lower(shifted(core_ref[0, size:, size:], g1), a_ref, t_ref)
        w_ref[size:, size:] = t1.T
        w_ref[:size, size:] = -exact(turned, exact(t1, c10), NT)

    device_sum(place, mine, *rest, first, second)
    for k in range(2):
        for h in range(2):
            for j in range(6):
                o_ref[pl.ds(128 * k + CHIPS * h, CHIPS), pl.ds(128 * j, 128)] = total[k, :, 2 * j + h, :]


def total_products(m, q, p):
    size = q.shape[0]
    half = size // 2
    return pl.pallas_call(
        total_kernel,
        out_shape=(jax.ShapeDtypeStruct(m.shape, f32), jax.ShapeDtypeStruct((size, size), f32)),
        in_specs=[pl.BlockSpec(memory_space=pltpu.VMEM)] * 3,
        out_specs=(pl.BlockSpec(memory_space=pltpu.VMEM),) * 2,
        scratch_shapes=[
            pltpu.VMEM((2, size, size), f32),
            pltpu.VMEM((half, half), f32),
            pltpu.VMEM((half, half), f32),
            *sum_scratch(12),
        ],
        compiler_params=pltpu.CompilerParams(collective_id=1, has_side_effects=True, vmem_limit_bytes=40 * MB),
    )(m, q, p)


def columns_kernel(r_ref, w_ref, m_ref, c_ref, g_ref, wh, wl, *, scale):
    @pl.when(pl.program_id(0) == 0)
    def _():
        w = w_ref[...]
        wh[...], wl[...] = halves(w)
        size = w.shape[0]
        wide = m_ref.shape[1] - size
        turned = w.T
        g_ref[:, :wide] = exact(turned, m_ref[:, :wide]) * scale
        g_ref[:, wide:] = exact(turned, exact(m_ref[:, wide:], w)) * scale

    rh, rl = halves(r_ref[...])
    c_ref[...] = mm(rh, wh[...]) + mm(rh, wl[...]) + mm(rl, wh[...])


def columns(r, w, m, tile=512):
    count, size = r.shape
    return pl.pallas_call(
        functools.partial(columns_kernel, scale=1.0 / count),
        out_shape=(jax.ShapeDtypeStruct(r.shape, f32), jax.ShapeDtypeStruct(m.shape, f32)),
        grid=(count // tile,),
        in_specs=[
            pl.BlockSpec((tile, size), lambda i: (i, 0)),
            pl.BlockSpec(w.shape, lambda i: (0, 0)),
            pl.BlockSpec(m.shape, lambda i: (0, 0)),
        ],
        out_specs=(pl.BlockSpec((tile, size), lambda i: (i, 0)), pl.BlockSpec(m.shape, lambda i: (0, 0))),
        scratch_shapes=[pltpu.VMEM(w.shape, bf16)] * 2,
        compiler_params=pltpu.CompilerParams(vmem_limit_bytes=40 * MB),
    )(r, w, m)


def body(points, factor, pivots):
    q, p = fetch(points, factor, pivots)
    r, m = residual(points, factor, q, p)
    m, w = total_products(m, q, p)
    return columns(r, w, m)


def solution(mesh):
    split = P(("row", "col"), None)
    return jax.shard_map(
        body,
        mesh=mesh,
        in_specs=(split, split, P()),
        out_specs=(split, P()),
        check_vma=False,
    )
```

```python
import functools

import jax
import jax.numpy as jnp
from jax import lax
from jax.experimental import pallas as pl
from jax.experimental.pallas import tpu as pltpu
from jax.sharding import PartitionSpec as P

f32 = jnp.float32
bf16 = jnp.bfloat16
MESH = pl.DeviceIdType.MESH
CHIPS = 64
NUGGET = 0.1
MB = 1 << 20

NT = (((1,), (1,)), ((), ()))
TN = (((0,), (0,)), ((), ()))
NN = (((1,), (0,)), ((), ()))


def exact(a, b, dims=NN):
    return lax.dot_general(a, b, dims, precision=lax.Precision.HIGHEST, preferred_element_type=f32)


def mm(a, b, dims=NN):
    return lax.dot_general(a, b, dims, preferred_element_type=f32)


def halves(a):
    high = a.astype(bf16)
    return high, (a - high.astype(f32)).astype(bf16)


def offsets():
    def hops(d):
        return sum(min(c, 4 - c) for c in (d // 16, d // 4 % 4, d % 4))

    return sorted(range(1, CHIPS), key=lambda d: (-hops(d), d))


class Place:
    def __init__(self):
        row, col = lax.axis_index("row"), lax.axis_index("col")
        self.core, z = row % 2, row // 2
        y, x = col // 4, col % 4
        self.chip = z * 16 + col
        self.number = row * 16 + col
        self.other = (row + 1 - 2 * self.core, col)
        zs = [(z + i) % 4 for i in range(4)]
        ys = [(y + i) % 4 for i in range(4)]
        xs = [(x + i) % 4 for i in range(4)]
        self.peers = []
        for d in offsets():
            pz, pc = zs[d // 16], ys[d // 4 % 4] * 4 + xs[d % 4]
            self.peers.append(((pz * 2 + self.core, pc), pz * 16 + pc))


def greet(place):
    barrier = pltpu.get_barrier_semaphore()
    for device, _ in place.peers:
        pl.semaphore_signal(barrier, inc=1, device_id=device, device_id_type=MESH)
    pl.semaphore_signal(barrier, inc=1, device_id=place.other, device_id_type=MESH)


def greeted():
    pl.semaphore_wait(pltpu.get_barrier_semaphore(), CHIPS)


def remote(src, dst, send, recv, device):
    return pltpu.make_async_remote_copy(src, dst, send, recv, device_id=device, device_id_type=MESH)


def device_sum(place, mine, pair, arrived, own, total, send, recv, work=None):
    core, chip, other = place.core, place.chip, place.other
    swap = remote(mine.at[1 - core], pair, send.at[0], recv.at[0], other)
    work = work or [lambda: None] * 4
    swap.start()
    work[0]()
    swap.wait_recv()
    pair[...] = mine[core] + pair[...]
    for slot, (device, target) in enumerate(place.peers):
        remote(pair.at[target], arrived.at[slot], send.at[1], recv.at[1], device).start()
    work[1]()
    remote(arrived, arrived, send.at[1], recv.at[1], other).wait_recv()
    own[...] = pair[chip] + jnp.sum(arrived[...], axis=0)
    for device, _ in place.peers:
        remote(own, total.at[core, chip], send.at[2], recv.at[2], device).start()
    total[core, chip] = own[...]
    work[2]()
    remote(arrived, arrived, send.at[2], recv.at[2], other).wait_recv()
    back = remote(total.at[core], total.at[core], send.at[3], recv.at[3], other)
    back.start()
    work[3]()
    swap.wait_send()
    remote(arrived, arrived, send.at[1], recv.at[1], other).wait_send()
    remote(arrived, arrived, send.at[2], recv.at[2], other).wait_send()
    back.wait()


def sum_scratch(rows):
    return [
        pltpu.VMEM((2, CHIPS, rows, 128), f32),
        pltpu.VMEM((CHIPS, rows, 128), f32),
        pltpu.VMEM((CHIPS - 1, rows, 128), f32),
        pltpu.VMEM((rows, 128), f32),
        pltpu.VMEM((2, CHIPS, rows, 128), f32),
        pltpu.SemaphoreType.DMA((4,)),
        pltpu.SemaphoreType.DMA((4,)),
    ]


def fetch_kernel(pivots_hbm, points_hbm, factor_hbm, q_ref, p_ref, pivots, turned, points, factor, load, mine, *rest):
    place = Place()
    loads = [
        pltpu.make_async_copy(points_hbm, turned, load.at[0]),
        pltpu.make_async_copy(pivots_hbm, pivots, load.at[1]),
        pltpu.make_async_copy(factor_hbm, factor, load.at[2]),
    ]
    for copy in loads:
        copy.start()
    greet(place)
    count = points.shape[0]
    first = place.number * count
    loads[0].wait()

    def turn(i, carry):
        at = pl.multiple_of(i * 128, 128)
        points[pl.ds(at, 128), :] = turned[:, pl.ds(at, 128)].T
        return carry

    lax.fori_loop(0, count // 128, turn, 0)
    loads[1].wait()
    loads[2].wait()

    def pick(i, carry):
        rows = []
        for s in range(2):
            local = pivots[s, i] - first
            inside = ((local >= 0) & (local < count)).astype(jnp.int32).astype(f32)
            local = jnp.clip(local, 0, count - 1)
            rows.append((points[pl.ds(local, 1), :] * inside, factor[pl.ds(local, 1), :] * inside))
        half, chip = i // CHIPS, i % CHIPS
        for s in range(2):
            for j in range(4):
                mine[half, chip, pl.ds(4 * s + j, 1), :] = rows[s][1][:, 128 * j : 128 * (j + 1)]
        mine[half, chip, pl.ds(8, 1), :] = jnp.concatenate([rows[0][0], rows[1][0]], axis=1)
        return carry

    lax.fori_loop(0, 2 * CHIPS, pick, 0, unroll=4)
    greeted()
    total = rest[3]
    device_sum(place, mine, *rest)
    for half in range(2):
        for s in range(2):
            for j in range(4):
                q_ref[pl.ds(128 * s + CHIPS * half, CHIPS), pl.ds(128 * j, 128)] = total[half, :, 4 * s + j, :]
        p_ref[pl.ds(CHIPS * half, CHIPS), :] = total[half, :, 8, :]


def fetch(points, factor, pivots):
    width, count = points.shape
    return pl.pallas_call(
        fetch_kernel,
        out_shape=(jax.ShapeDtypeStruct((256, 512), f32), jax.ShapeDtypeStruct((128, 128), f32)),
        in_specs=[pl.BlockSpec(memory_space=pltpu.HBM)] * 3,
        out_specs=(pl.BlockSpec(memory_space=pltpu.VMEM), pl.BlockSpec(memory_space=pltpu.VMEM)),
        scratch_shapes=[
            pltpu.SMEM(pivots.shape, jnp.int32),
            pltpu.VMEM((width, count), f32),
            pltpu.VMEM((count, width), f32),
            pltpu.VMEM(factor.shape, f32),
            pltpu.SemaphoreType.DMA((3,)),
            *sum_scratch(9),
        ],
        compiler_params=pltpu.CompilerParams(collective_id=0, has_side_effects=True, vmem_limit_bytes=51 * MB),
    )(pivots, points, factor)


def residual_kernel(points, factor, q_ref, p_ref, r_ref, m_ref, qh, ql, pt, pn, cross, xa, ra, xb, rb):
    step = pl.program_id(0)
    width = points.shape[0]
    tile, wide = factor.shape[0] // 2, factor.shape[1]

    @pl.when(step == 0)
    def _():
        qh[...], ql[...] = halves(q_ref[...].T)
        pp = p_ref[...].T
        p = jnp.concatenate([pp[:width], pp[width:]], axis=1) * (2.0 / width)
        high, low = halves(p)
        pt[...] = jnp.concatenate([high, low, high, low], axis=0)
        pn[...] = jnp.sum(p * p, axis=0, keepdims=True) * (width / 4.0)
        for ref in (m_ref, cross, xb, rb):
            ref[...] = jnp.zeros_like(ref)

    def make(first, x, r):
        a = points[:, first : first + tile]
        high, low = halves(a)
        inner = mm(jnp.concatenate([high, high, low, low], axis=0), pt[...], TN)
        norm = jnp.sum(a * a, axis=0, keepdims=True) * (1.0 / width)
        norm = jnp.broadcast_to(norm, (8, tile)).T[:, :1]
        xh, xl = halves(factor[first : first + tile, :])
        value = jnp.exp(inner - norm - pn[...]) - (mm(xh, qh[...]) + mm(xh, ql[...]) + mm(xl, qh[...]))
        r_ref[first : first + tile, :] = value
        x[0], x[1] = xh, xl
        r[0], r[1] = halves(value)

    def add(x, r):
        rh, rl = r[0], r[1]
        m_ref[:, :wide] += mm(rh, x[0], TN) + mm(rh, x[1], TN) + mm(rl, x[0], TN)
        m_ref[:, wide:] += mm(rh, rh, TN)
        cross[...] += mm(rh, rl, TN)

    add(xb, rb)
    make(0, xa, ra)
    add(xa, ra)
    make(tile, xb, rb)

    @pl.when(step == pl.num_programs(0) - 1)
    def _():
        add(xb, rb)
        m_ref[:, wide:] += cross[...] + cross[...].T


def residual(points, factor, q, p, tile=512):
    width, count = points.shape
    wide = factor.shape[1]
    size = q.shape[0]
    return pl.pallas_call(
        residual_kernel,
        out_shape=(jax.ShapeDtypeStruct((count, size), f32), jax.ShapeDtypeStruct((size, wide + size), f32)),
        grid=(count // tile,),
        in_specs=[
            pl.BlockSpec((width, tile), lambda i: (0, i)),
            pl.BlockSpec((tile, wide), lambda i: (i, 0)),
            pl.BlockSpec(q.shape, lambda i: (0, 0)),
            pl.BlockSpec(p.shape, lambda i: (0, 0)),
        ],
        out_specs=(
            pl.BlockSpec((tile, size), lambda i: (i, 0)),
            pl.BlockSpec((size, wide + size), lambda i: (0, 0)),
        ),
        scratch_shapes=[
            pltpu.VMEM((wide, size), bf16),
            pltpu.VMEM((wide, size), bf16),
            pltpu.VMEM((4 * width, size), bf16),
            pltpu.VMEM((1, size), f32),
            pltpu.VMEM((size, size), f32),
            *[pltpu.VMEM((2, tile // 2, wide), bf16), pltpu.VMEM((2, tile // 2, size), bf16)] * 2,
        ],
        compiler_params=pltpu.CompilerParams(vmem_limit_bytes=40 * MB),
    )(points, factor, q, p)


def spread(a, rows):
    return jnp.broadcast_to(a, (rows, 128))


def panel_factor(block):
    columns = [spread(block[:, i : i + 1], 8) for i in range(8)]
    left = {(i, j): spread(columns[j][i : i + 1, :], 8) for i in range(8) for j in range(i, 8)}
    lower, inverse = {}, {}
    for i in range(8):
        scale = lax.rsqrt(left[i, i])
        for j in range(i + 1, 8):
            lower[j, i] = left[i, j] * scale
        for j in range(i + 1, 8):
            for k in range(j, 8):
                left[j, k] = left[j, k] - lower[j, i] * lower[k, i]
        inverse[i, i] = scale
        for j in range(i):
            terms = [lower[i, k] * inverse[k, j] for k in range(j, i)]
            inverse[i, j] = -functools.reduce(jnp.add, terms) * scale
    row = lax.broadcasted_iota(jnp.int32, (8, 128), 0)
    made = []
    for j in range(8):
        column = jnp.zeros((8, 128), f32)
        for i in range(j, 8):
            column = jnp.where(row == i, inverse[i, j], column)
        made.append(column)
    return made


def thirds(a):
    high = a.astype(bf16).astype(f32)
    middle = (a - high).astype(bf16).astype(f32)
    return high, middle, a - high - middle


def inverse_lower(core, a_ref, t_ref):
    size = core.shape[0]
    rows = lax.broadcasted_iota(jnp.int32, (size, size), 0)
    cols = lax.broadcasted_iota(jnp.int32, (size, size), 1)
    a_ref[...] = core
    t_ref[...] = (rows == cols).astype(f32)

    def step(b, carry):
        first = pl.multiple_of(b * 8, 8)
        line, made = a_ref[pl.ds(first, 8), :], t_ref[pl.ds(first, 8), :]
        factors = panel_factor(pltpu.roll(line, lax.rem(size - first, size), 1))
        line = functools.reduce(jnp.add, [f * spread(line[i : i + 1, :], 8) for i, f in enumerate(factors)])
        made = functools.reduce(jnp.add, [f * spread(made[i : i + 1, :], 8) for i, f in enumerate(factors)])
        t_ref[pl.ds(first, 8), :] = made
        high, middle, low = thirds(jnp.concatenate([line, made], axis=1))
        right = jnp.concatenate([high, middle, high, middle, low, high], axis=0)
        left = jnp.concatenate([high, high, middle, middle, high, low], axis=0)[:, :size]
        change = mm(left.astype(bf16), right.astype(bf16), TN)
        a_ref[...] = a_ref[...] - change[:, :size]
        t_ref[...] = t_ref[...] - jnp.where(rows >= first + 8, change[:, size:], 0.0)
        return carry

    lax.fori_loop(0, size // 8, step, 0)
    return t_ref[...]


def pivot_terms(q_ref, p_ref, core_ref):
    q = q_ref[...]
    pp = p_ref[...]
    width = pp.shape[1] // 2
    p = jnp.concatenate([pp[:, :width], pp[:, width:]], axis=0)
    norm = jnp.sum(p * p, axis=1, keepdims=True)
    across = exact(jnp.ones((8, width), f32), p * p, NT)[:1]
    core_ref[0] = jnp.exp((2.0 * exact(p, p, NT) - norm - across) * (1.0 / width))
    core_ref[1] = exact(q, q, NT)


def shifted(k, g):
    rows = lax.broadcasted_iota(jnp.int32, g.shape, 0)
    cols = lax.broadcasted_iota(jnp.int32, g.shape, 1)
    shift = NUGGET + jnp.max(jnp.sum(jnp.abs(g), axis=1, keepdims=True), axis=0, keepdims=True)
    return k - g + shift * (rows == cols).astype(f32)


def total_kernel(m_ref, q_ref, p_ref, o_ref, w_ref, core_ref, a_ref, t_ref, c_ref, mine, *rest):
    place = Place()
    greet(place)
    for k in range(2):
        for h in range(2):
            for j in range(6):
                mine[k, :, 2 * j + h, :] = m_ref[pl.ds(128 * k + CHIPS * h, CHIPS), pl.ds(128 * j, 128)]
    greeted()
    total = rest[3]
    size = a_ref.shape[0]

    def terms():
        pivot_terms(q_ref, p_ref, core_ref)

    def first():
        t0 = inverse_lower(shifted(core_ref[0, :size, :size], core_ref[1, :size, :size]), a_ref, t_ref)
        w_ref[:size, :size] = t0.T
        w_ref[size:, :size] = jnp.zeros((size, size), f32)

    def second():
        turned = w_ref[:size, :size]
        c10 = exact(core_ref[0, size:, :size] - core_ref[1, size:, :size], turned)
        g1 = core_ref[1, size:, size:] + exact(c10, c10, NT)
        t1 = inverse_lower(shifted(core_ref[0, size:, size:], g1), a_ref, t_ref)
        w_ref[size:, size:] = t1.T
        c_ref[...] = c10

    def third():
        w_ref[:size, size:] = -exact(w_ref[:size, :size], exact(t_ref[...], c_ref[...]), NT)

    device_sum(place, mine, *rest, [terms, first, second, third])
    for k in range(2):
        for h in range(2):
            for j in range(6):
                o_ref[pl.ds(128 * k + CHIPS * h, CHIPS), pl.ds(128 * j, 128)] = total[k, :, 2 * j + h, :]


def total_products(m, q, p):
    size = q.shape[0]
    half = size // 2
    return pl.pallas_call(
        total_kernel,
        out_shape=(jax.ShapeDtypeStruct(m.shape, f32), jax.ShapeDtypeStruct((size, size), f32)),
        in_specs=[pl.BlockSpec(memory_space=pltpu.VMEM)] * 3,
        out_specs=(pl.BlockSpec(memory_space=pltpu.VMEM),) * 2,
        scratch_shapes=[
            pltpu.VMEM((2, size, size), f32),
            *[pltpu.VMEM((half, half), f32)] * 3,
            *sum_scratch(12),
        ],
        compiler_params=pltpu.CompilerParams(collective_id=1, has_side_effects=True, vmem_limit_bytes=40 * MB),
    )(m, q, p)


def columns_kernel(r_ref, w_ref, m_ref, c_ref, g_ref, wh, wl, *, scale):
    @pl.when(pl.program_id(0) == 0)
    def _():
        w = w_ref[...]
        wh[...], wl[...] = halves(w)
        size = w.shape[0]
        wide = m_ref.shape[1] - size
        turned = w.T
        g_ref[:, :wide] = exact(turned, m_ref[:, :wide]) * scale
        g_ref[:, wide:] = exact(turned, exact(m_ref[:, wide:], w)) * scale

    rh, rl = halves(r_ref[...])
    c_ref[...] = mm(rh, wh[...]) + mm(rh, wl[...]) + mm(rl, wh[...])


def columns(r, w, m, tile=512):
    count, size = r.shape
    return pl.pallas_call(
        functools.partial(columns_kernel, scale=1.0 / count),
        out_shape=(jax.ShapeDtypeStruct(r.shape, f32), jax.ShapeDtypeStruct(m.shape, f32)),
        grid=(count // tile,),
        in_specs=[
            pl.BlockSpec((tile, size), lambda i: (i, 0)),
            pl.BlockSpec(w.shape, lambda i: (0, 0)),
            pl.BlockSpec(m.shape, lambda i: (0, 0)),
        ],
        out_specs=(pl.BlockSpec((tile, size), lambda i: (i, 0)), pl.BlockSpec(m.shape, lambda i: (0, 0))),
        scratch_shapes=[pltpu.VMEM(w.shape, bf16)] * 2,
        compiler_params=pltpu.CompilerParams(vmem_limit_bytes=40 * MB),
    )(r, w, m)


def body(points, factor, pivots):
    points = points.T
    q, p = fetch(points, factor, pivots)
    r, m = residual(points, factor, q, p)
    m, w = total_products(m, q, p)
    return columns(r, w, m)


def solution(mesh):
    split = P(("row", "col"), None)
    return jax.shard_map(
        body,
        mesh=mesh,
        in_specs=(split, split, P()),
        out_specs=(split, P()),
        check_vma=False,
    )
```

```python
import functools

import jax
import jax.numpy as jnp
from jax import lax
from jax.experimental import pallas as pl
from jax.experimental.pallas import tpu as pltpu
from jax.sharding import PartitionSpec as P

f32 = jnp.float32
bf16 = jnp.bfloat16
MESH = pl.DeviceIdType.MESH
CHIPS = 64
NUGGET = 0.1
MB = 1 << 20

NT = (((1,), (1,)), ((), ()))
TN = (((0,), (0,)), ((), ()))
NN = (((1,), (0,)), ((), ()))


def exact(a, b, dims=NN):
    return lax.dot_general(a, b, dims, precision=lax.Precision.HIGHEST, preferred_element_type=f32)


def mm(a, b, dims=NN):
    return lax.dot_general(a, b, dims, preferred_element_type=f32)


def halves(a):
    high = a.astype(bf16)
    return high, (a - high.astype(f32)).astype(bf16)


PLANES = (2, 1, 3, 0)


def offsets(plane):
    def hops(d):
        return sum(min(c, 4 - c) for c in (d // 4, d % 4))

    return sorted(range(0 if plane else 1, 16), key=lambda d: (-hops(d), d))


class Place:
    def __init__(self):
        row, col = lax.axis_index("row"), lax.axis_index("col")
        self.core, z = row % 2, row // 2
        y, x = col // 4, col % 4
        self.chip = z * 16 + col
        self.number = row * 16 + col
        self.other = (row + 1 - 2 * self.core, col)
        zs = [(z + i) % 4 for i in range(4)]
        ys = [(y + i) % 4 for i in range(4)]
        xs = [(x + i) % 4 for i in range(4)]
        self.ahead = [pl.multiple_of(z * 16, 16) for z in zs]
        self.peers = {}
        for plane in PLANES:
            made = []
            for d in offsets(plane):
                at = ys[d // 4] * 4 + xs[d % 4]
                made.append(((zs[plane] * 2 + self.core, at), zs[plane] * 16 + at))
            self.peers[plane] = made


def greet(place):
    barrier = pltpu.get_barrier_semaphore()
    for plane in PLANES:
        for device, _ in place.peers[plane]:
            pl.semaphore_signal(barrier, inc=1, device_id=device, device_id_type=MESH)
    pl.semaphore_signal(barrier, inc=1, device_id=place.other, device_id_type=MESH)


def greeted():
    pl.semaphore_wait(pltpu.get_barrier_semaphore(), CHIPS)


def remote(src, dst, send, recv, device):
    return pltpu.make_async_remote_copy(src, dst, send, recv, device_id=device, device_id_type=MESH)


def device_sum(place, mine, pair, arrived, own, total, send, recv, work=None):
    core, chip, other = place.core, place.chip, place.other
    work = work or [lambda: None] * 4
    swaps = {}
    for plane in PLANES:
        at = pl.ds(place.ahead[plane], 16)
        swaps[plane] = remote(mine.at[1 - core, at], pair.at[at], send.at[plane], recv.at[plane], other)
        swaps[plane].start()
    work[0]()
    slot = 0
    for plane in PLANES:
        at = pl.ds(place.ahead[plane], 16)
        swaps[plane].wait_recv()
        pair[at] = mine[core, at] + pair[at]
        for device, target in place.peers[plane]:
            remote(pair.at[target], arrived.at[slot], send.at[4], recv.at[4], device).start()
            slot += 1
    work[1]()
    remote(arrived, arrived, send.at[4], recv.at[4], other).wait_recv()
    own[...] = pair[chip] + jnp.sum(arrived[...], axis=0)
    for plane in PLANES:
        for device, _ in place.peers[plane]:
            remote(own, total.at[core, chip], send.at[5 + plane], recv.at[5 + plane], device).start()
    total[core, chip] = own[...]
    work[2]()
    backs = []
    for plane in reversed(PLANES):
        some = arrived.at[pl.ds(0, 16 if plane else 15)]
        remote(some, some, send.at[5 + plane], recv.at[5 + plane], other).wait_recv()
        block = total.at[core, pl.ds(place.ahead[-plane % 4], 16)]
        backs.append(remote(block, block, send.at[9 + plane], recv.at[9 + plane], other))
        backs[-1].start()
    work[3]()
    for plane in PLANES:
        swaps[plane].wait_send()
    remote(arrived, arrived, send.at[4], recv.at[4], other).wait_send()
    for plane in PLANES:
        some = arrived.at[pl.ds(0, 16 if plane else 15)]
        remote(some, some, send.at[5 + plane], recv.at[5 + plane], other).wait_send()
    for back in backs:
        back.wait()


def sum_scratch(rows):
    return [
        pltpu.VMEM((2, CHIPS, rows, 128), f32),
        pltpu.VMEM((CHIPS, rows, 128), f32),
        pltpu.VMEM((CHIPS - 1, rows, 128), f32),
        pltpu.VMEM((rows, 128), f32),
        pltpu.VMEM((2, CHIPS, rows, 128), f32),
        pltpu.SemaphoreType.DMA((13,)),
        pltpu.SemaphoreType.DMA((13,)),
    ]


def fetch_kernel(pivots_hbm, points_hbm, factor_hbm, q_ref, p_ref, pivots, turned, points, factor, load, mine, *rest):
    place = Place()
    loads = [
        pltpu.make_async_copy(points_hbm, turned, load.at[0]),
        pltpu.make_async_copy(pivots_hbm, pivots, load.at[1]),
        pltpu.make_async_copy(factor_hbm, factor, load.at[2]),
    ]
    for copy in loads:
        copy.start()
    greet(place)
    count = points.shape[0]
    first = place.number * count
    loads[0].wait()

    def turn(i, carry):
        at = pl.multiple_of(i * 128, 128)
        points[pl.ds(at, 128), :] = turned[:, pl.ds(at, 128)].T
        return carry

    lax.fori_loop(0, count // 128, turn, 0)
    loads[1].wait()
    loads[2].wait()

    def pick(i, carry):
        rows = []
        for s in range(2):
            local = pivots[s, i] - first
            inside = ((local >= 0) & (local < count)).astype(jnp.int32).astype(f32)
            local = jnp.clip(local, 0, count - 1)
            rows.append((points[pl.ds(local, 1), :] * inside, factor[pl.ds(local, 1), :] * inside))
        half, chip = i // CHIPS, i % CHIPS
        for s in range(2):
            for j in range(4):
                mine[half, chip, pl.ds(4 * s + j, 1), :] = rows[s][1][:, 128 * j : 128 * (j + 1)]
        mine[half, chip, pl.ds(8, 1), :] = jnp.concatenate([rows[0][0], rows[1][0]], axis=1)
        return carry

    lax.fori_loop(0, 2 * CHIPS, pick, 0, unroll=4)
    greeted()
    total = rest[3]
    device_sum(place, mine, *rest)
    for half in range(2):
        for s in range(2):
            for j in range(4):
                q_ref[pl.ds(128 * s + CHIPS * half, CHIPS), pl.ds(128 * j, 128)] = total[half, :, 4 * s + j, :]
        p_ref[pl.ds(CHIPS * half, CHIPS), :] = total[half, :, 8, :]


def fetch(points, factor, pivots):
    width, count = points.shape
    return pl.pallas_call(
        fetch_kernel,
        out_shape=(jax.ShapeDtypeStruct((256, 512), f32), jax.ShapeDtypeStruct((128, 128), f32)),
        in_specs=[pl.BlockSpec(memory_space=pltpu.HBM)] * 3,
        out_specs=(pl.BlockSpec(memory_space=pltpu.VMEM), pl.BlockSpec(memory_space=pltpu.VMEM)),
        scratch_shapes=[
            pltpu.SMEM(pivots.shape, jnp.int32),
            pltpu.VMEM((width, count), f32),
            pltpu.VMEM((count, width), f32),
            pltpu.VMEM(factor.shape, f32),
            pltpu.SemaphoreType.DMA((3,)),
            *sum_scratch(9),
        ],
        compiler_params=pltpu.CompilerParams(collective_id=0, has_side_effects=True, vmem_limit_bytes=51 * MB),
    )(pivots, points, factor)


def residual_kernel(points, factor, q_ref, p_ref, r_ref, m_ref, qh, ql, pt, pn, turned, cross, xa, ra, xb, rb):
    step = pl.program_id(0)
    width = points.shape[0]
    tile, wide = factor.shape[0] // 2, factor.shape[1]

    @pl.when(step == 0)
    def _():
        qh[...], ql[...] = halves(q_ref[...].T)
        pp = p_ref[...].T
        p = jnp.concatenate([pp[:width], pp[width:]], axis=1) * (2.0 / width)
        high, low = halves(p)
        pt[...] = jnp.concatenate([high, low, high, low], axis=0)
        pn[...] = jnp.sum(p * p, axis=0, keepdims=True) * (width / 4.0)
        for ref in (turned, cross, xb, rb):
            ref[...] = jnp.zeros_like(ref)

    def make(first, x, r):
        a = points[:, first : first + tile]
        high, low = halves(a)
        inner = mm(jnp.concatenate([high, high, low, low], axis=0), pt[...], TN)
        norm = jnp.sum(a * a, axis=0, keepdims=True) * (1.0 / width)
        norm = jnp.broadcast_to(norm, (8, tile)).T[:, :1]
        xh, xl = halves(factor[first : first + tile, :])
        value = jnp.exp(inner - norm - pn[...]) - (mm(xh, qh[...]) + mm(xh, ql[...]) + mm(xl, qh[...]))
        r_ref[first : first + tile, :] = value
        x[0], x[1] = xh, xl
        r[0], r[1] = halves(value)

    def add(x, r):
        rh, rl = r[0], r[1]
        size = rh.shape[1]
        both = mm(jnp.concatenate([x[0], x[1], rh, rl], axis=1), rh, TN)
        turned[:wide, :] += both[:wide] + both[wide : 2 * wide] + mm(x[0], rl, TN)
        turned[wide:, :] += both[2 * wide : 2 * wide + size]
        cross[...] += both[2 * wide + size :]

    add(xb, rb)
    make(0, xa, ra)
    add(xa, ra)
    make(tile, xb, rb)

    @pl.when(step == pl.num_programs(0) - 1)
    def _():
        add(xb, rb)
        m_ref[:, :wide] = turned[:wide, :].T
        m_ref[:, wide:] = turned[wide:, :] + cross[...] + cross[...].T


def residual(points, factor, q, p, tile=1024):
    width, count = points.shape
    wide = factor.shape[1]
    size = q.shape[0]
    return pl.pallas_call(
        residual_kernel,
        out_shape=(jax.ShapeDtypeStruct((count, size), f32), jax.ShapeDtypeStruct((size, wide + size), f32)),
        grid=(count // tile,),
        in_specs=[
            pl.BlockSpec((width, tile), lambda i: (0, i)),
            pl.BlockSpec((tile, wide), lambda i: (i, 0)),
            pl.BlockSpec(q.shape, lambda i: (0, 0)),
            pl.BlockSpec(p.shape, lambda i: (0, 0)),
        ],
        out_specs=(
            pl.BlockSpec((tile, size), lambda i: (i, 0)),
            pl.BlockSpec((size, wide + size), lambda i: (0, 0)),
        ),
        scratch_shapes=[
            pltpu.VMEM((wide, size), bf16),
            pltpu.VMEM((wide, size), bf16),
            pltpu.VMEM((4 * width, size), bf16),
            pltpu.VMEM((1, size), f32),
            pltpu.VMEM((wide + size, size), f32),
            pltpu.VMEM((size, size), f32),
            *[pltpu.VMEM((2, tile // 2, wide), bf16), pltpu.VMEM((2, tile // 2, size), bf16)] * 2,
        ],
        compiler_params=pltpu.CompilerParams(vmem_limit_bytes=40 * MB),
    )(points, factor, q, p)


def spread(a, rows):
    return jnp.broadcast_to(a, (rows, 128))


def panel_factor(block):
    columns = [spread(block[:, i : i + 1], 8) for i in range(8)]
    left = {(i, j): spread(columns[j][i : i + 1, :], 8) for i in range(8) for j in range(i, 8)}
    lower, inverse = {}, {}
    for i in range(8):
        scale = lax.rsqrt(left[i, i])
        for j in range(i + 1, 8):
            lower[j, i] = left[i, j] * scale
        for j in range(i + 1, 8):
            for k in range(j, 8):
                left[j, k] = left[j, k] - lower[j, i] * lower[k, i]
        inverse[i, i] = scale
        for j in range(i):
            terms = [lower[i, k] * inverse[k, j] for k in range(j, i)]
            inverse[i, j] = -functools.reduce(jnp.add, terms) * scale
    row = lax.broadcasted_iota(jnp.int32, (8, 128), 0)
    made = []
    for j in range(8):
        column = jnp.zeros((8, 128), f32)
        for i in range(j, 8):
            column = jnp.where(row == i, inverse[i, j], column)
        made.append(column)
    return made


def thirds(a):
    high = a.astype(bf16).astype(f32)
    middle = (a - high).astype(bf16).astype(f32)
    return high, middle, a - high - middle


def begin_inverse(core, a_ref, t_ref):
    rows = lax.broadcasted_iota(jnp.int32, core.shape, 0)
    cols = lax.broadcasted_iota(jnp.int32, core.shape, 1)
    a_ref[...] = core
    t_ref[...] = (rows == cols).astype(f32)


def run_inverse(a_ref, t_ref, start, stop):
    size = a_ref.shape[0]
    rows = lax.broadcasted_iota(jnp.int32, (size, size), 0)

    def step(b, carry):
        first = pl.multiple_of(b * 8, 8)
        line, made = a_ref[pl.ds(first, 8), :], t_ref[pl.ds(first, 8), :]
        factors = panel_factor(pltpu.roll(line, lax.rem(size - first, size), 1))
        line = functools.reduce(jnp.add, [f * spread(line[i : i + 1, :], 8) for i, f in enumerate(factors)])
        made = functools.reduce(jnp.add, [f * spread(made[i : i + 1, :], 8) for i, f in enumerate(factors)])
        t_ref[pl.ds(first, 8), :] = made
        high, middle, low = thirds(jnp.concatenate([line, made], axis=1))
        right = jnp.concatenate([high, middle, high, middle, low, high], axis=0)
        left = jnp.concatenate([high, high, middle, middle, high, low], axis=0)[:, :size]
        change = mm(left.astype(bf16), right.astype(bf16), TN)
        a_ref[...] = a_ref[...] - change[:, :size]
        t_ref[...] = t_ref[...] - jnp.where(rows >= first + 8, change[:, size:], 0.0)
        return carry

    lax.fori_loop(start, stop, step, 0)


def pivot_terms(q_ref, p_ref, core_ref):
    q = q_ref[...]
    pp = p_ref[...]
    width = pp.shape[1] // 2
    p = jnp.concatenate([pp[:, :width], pp[:, width:]], axis=0)
    norm = jnp.sum(p * p, axis=1, keepdims=True)
    across = exact(jnp.ones((8, width), f32), p * p, NT)[:1]
    core_ref[0] = jnp.exp((2.0 * exact(p, p, NT) - norm - across) * (1.0 / width))
    core_ref[1] = exact(q, q, NT)


def shifted(k, g):
    rows = lax.broadcasted_iota(jnp.int32, g.shape, 0)
    cols = lax.broadcasted_iota(jnp.int32, g.shape, 1)
    shift = NUGGET + jnp.max(jnp.sum(jnp.abs(g), axis=1, keepdims=True), axis=0, keepdims=True)
    return k - g + shift * (rows == cols).astype(f32)


def total_kernel(m_ref, q_ref, p_ref, o_ref, w_ref, core_ref, a_ref, t_ref, c_ref, mine, *rest):
    place = Place()
    greet(place)
    for k in range(2):
        for h in range(2):
            for j in range(6):
                mine[k, :, 2 * j + h, :] = m_ref[pl.ds(128 * k + CHIPS * h, CHIPS), pl.ds(128 * j, 128)]
    greeted()
    total = rest[3]
    size = a_ref.shape[0]

    def during_swap():
        pivot_terms(q_ref, p_ref, core_ref)
        begin_inverse(shifted(core_ref[0, :size, :size], core_ref[1, :size, :size]), a_ref, t_ref)

    def during_scatter():
        run_inverse(a_ref, t_ref, 0, 12)

    def during_gather():
        run_inverse(a_ref, t_ref, 12, 16)
        turned = t_ref[...].T
        w_ref[:size, :size] = turned
        w_ref[size:, :size] = jnp.zeros((size, size), f32)
        c10 = exact(core_ref[0, size:, :size] - core_ref[1, size:, :size], turned)
        c_ref[...] = c10
        g1 = core_ref[1, size:, size:] + exact(c10, c10, NT)
        begin_inverse(shifted(core_ref[0, size:, size:], g1), a_ref, t_ref)
        run_inverse(a_ref, t_ref, 0, 8)

    def on_the_way_back():
        run_inverse(a_ref, t_ref, 8, 16)
        t1 = t_ref[...]
        w_ref[size:, size:] = t1.T
        w_ref[:size, size:] = -exact(w_ref[:size, :size], exact(t1, c_ref[...]), NT)

    device_sum(place, mine, *rest, [during_swap, during_scatter, during_gather, on_the_way_back])
    for k in range(2):
        for h in range(2):
            for j in range(6):
                o_ref[pl.ds(128 * k + CHIPS * h, CHIPS), pl.ds(128 * j, 128)] = total[k, :, 2 * j + h, :]


def total_products(m, q, p):
    size = q.shape[0]
    half = size // 2
    return pl.pallas_call(
        total_kernel,
        out_shape=(jax.ShapeDtypeStruct(m.shape, f32), jax.ShapeDtypeStruct((size, size), f32)),
        in_specs=[pl.BlockSpec(memory_space=pltpu.VMEM)] * 3,
        out_specs=(pl.BlockSpec(memory_space=pltpu.VMEM),) * 2,
        scratch_shapes=[
            pltpu.VMEM((2, size, size), f32),
            *[pltpu.VMEM((half, half), f32)] * 3,
            *sum_scratch(12),
        ],
        compiler_params=pltpu.CompilerParams(collective_id=1, has_side_effects=True, vmem_limit_bytes=40 * MB),
    )(m, q, p)


def product(a, b):
    ah, al = halves(a)
    bh, bl = halves(b)
    both = mm(jnp.concatenate([ah, al], axis=0), bh)
    return both[: len(a)] + both[len(a) :] + mm(ah, bl)


def columns_kernel(r_ref, w_ref, m_ref, c_ref, g_ref, *, scale):
    w = w_ref[...]
    c_ref[...] = product(r_ref[...], w)

    @pl.when(pl.program_id(0) == pl.num_programs(0) - 1)
    def _():
        size = w.shape[0]
        wide = m_ref.shape[1] - size
        right = product(m_ref[:, wide:], w)
        g_ref[...] = product(w.T, jnp.concatenate([m_ref[:, :wide], right], axis=1)) * scale


def columns(r, w, m, tile=1024):
    count, size = r.shape
    return pl.pallas_call(
        functools.partial(columns_kernel, scale=1.0 / count),
        out_shape=(jax.ShapeDtypeStruct(r.shape, f32), jax.ShapeDtypeStruct(m.shape, f32)),
        grid=(count // tile,),
        in_specs=[
            pl.BlockSpec((tile, size), lambda i: (i, 0)),
            pl.BlockSpec(w.shape, lambda i: (0, 0)),
            pl.BlockSpec(m.shape, lambda i: (0, 0)),
        ],
        out_specs=(pl.BlockSpec((tile, size), lambda i: (i, 0)), pl.BlockSpec(m.shape, lambda i: (0, 0))),
        compiler_params=pltpu.CompilerParams(vmem_limit_bytes=40 * MB),
    )(r, w, m)


def body(points, factor, pivots):
    points = points.T
    q, p = fetch(points, factor, pivots)
    r, m = residual(points, factor, q, p)
    m, w = total_products(m, q, p)
    return columns(r, w, m)


def solution(mesh):
    split = P(("row", "col"), None)
    return jax.shard_map(
        body,
        mesh=mesh,
        in_specs=(split, split, P()),
        out_specs=(split, P()),
        check_vma=False,
    )
```

```python
import functools

import jax
import jax.numpy as jnp
from jax import lax
from jax.experimental import pallas as pl
from jax.experimental.pallas import tpu as pltpu
from jax.sharding import PartitionSpec as P

f32 = jnp.float32
bf16 = jnp.bfloat16
MESH = pl.DeviceIdType.MESH
CHIPS = 64
NUGGET = 0.1
MB = 1 << 20

NT = (((1,), (1,)), ((), ()))
TN = (((0,), (0,)), ((), ()))
NN = (((1,), (0,)), ((), ()))


def exact(a, b, dims=NN):
    return lax.dot_general(a, b, dims, precision=lax.Precision.HIGHEST, preferred_element_type=f32)


def mm(a, b, dims=NN):
    return lax.dot_general(a, b, dims, preferred_element_type=f32)


def halves(a):
    high = a.astype(bf16)
    return high, (a - high.astype(f32)).astype(bf16)


PLANES = (2, 1, 3, 0)


def offsets(plane):
    def hops(d):
        return sum(min(c, 4 - c) for c in (d // 4, d % 4))

    return sorted(range(0 if plane else 1, 16), key=lambda d: (-hops(d), d))


class Place:
    def __init__(self):
        row, col = lax.axis_index("row"), lax.axis_index("col")
        self.core, z = row % 2, row // 2
        y, x = col // 4, col % 4
        self.chip = z * 16 + col
        self.number = row * 16 + col
        self.other = (row + 1 - 2 * self.core, col)
        zs = [(z + i) % 4 for i in range(4)]
        ys = [(y + i) % 4 for i in range(4)]
        xs = [(x + i) % 4 for i in range(4)]
        self.ahead = [pl.multiple_of(z * 16, 16) for z in zs]
        self.peers = {}
        for plane in PLANES:
            made = []
            for d in offsets(plane):
                at = ys[d // 4] * 4 + xs[d % 4]
                made.append(((zs[plane] * 2 + self.core, at), zs[plane] * 16 + at))
            self.peers[plane] = made


def greet(place):
    barrier = pltpu.get_barrier_semaphore()
    for plane in PLANES:
        for device, _ in place.peers[plane]:
            pl.semaphore_signal(barrier, inc=1, device_id=device, device_id_type=MESH)
    pl.semaphore_signal(barrier, inc=1, device_id=place.other, device_id_type=MESH)


def greeted():
    pl.semaphore_wait(pltpu.get_barrier_semaphore(), CHIPS)


def remote(src, dst, send, recv, device):
    return pltpu.make_async_remote_copy(src, dst, send, recv, device_id=device, device_id_type=MESH)


def device_sum(place, mine, pair, arrived, own, total, send, recv, work=None):
    core, chip, other = place.core, place.chip, place.other
    work = work or [lambda: None] * 4
    swaps = {}
    for plane in PLANES:
        at = pl.ds(place.ahead[plane], 16)
        swaps[plane] = remote(mine.at[1 - core, at], pair.at[at], send.at[plane], recv.at[plane], other)
        swaps[plane].start()
    work[0]()
    slot = 0
    for plane in PLANES:
        at = pl.ds(place.ahead[plane], 16)
        swaps[plane].wait_recv()
        pair[at] = mine[core, at] + pair[at]
        for device, target in place.peers[plane]:
            remote(pair.at[target], arrived.at[slot], send.at[4], recv.at[4], device).start()
            slot += 1
    work[1]()
    remote(arrived, arrived, send.at[4], recv.at[4], other).wait_recv()
    own[...] = pair[chip] + jnp.sum(arrived[...], axis=0)
    for plane in PLANES:
        for device, _ in place.peers[plane]:
            remote(own, total.at[core, chip], send.at[5 + plane], recv.at[5 + plane], device).start()
    total[core, chip] = own[...]
    work[2]()
    backs = []
    for plane in reversed(PLANES):
        some = arrived.at[pl.ds(0, 16 if plane else 15)]
        remote(some, some, send.at[5 + plane], recv.at[5 + plane], other).wait_recv()
        block = total.at[core, pl.ds(place.ahead[-plane % 4], 16)]
        backs.append(remote(block, block, send.at[9 + plane], recv.at[9 + plane], other))
        backs[-1].start()
    work[3]()
    for plane in PLANES:
        swaps[plane].wait_send()
    remote(arrived, arrived, send.at[4], recv.at[4], other).wait_send()
    for plane in PLANES:
        some = arrived.at[pl.ds(0, 16 if plane else 15)]
        remote(some, some, send.at[5 + plane], recv.at[5 + plane], other).wait_send()
    for back in backs:
        back.wait()


def sum_scratch(rows):
    return [
        pltpu.VMEM((2, CHIPS, rows, 128), f32),
        pltpu.VMEM((CHIPS, rows, 128), f32),
        pltpu.VMEM((CHIPS - 1, rows, 128), f32),
        pltpu.VMEM((rows, 128), f32),
        pltpu.VMEM((2, CHIPS, rows, 128), f32),
        pltpu.SemaphoreType.DMA((13,)),
        pltpu.SemaphoreType.DMA((13,)),
    ]


def spread(a, rows):
    return jnp.broadcast_to(a, (rows, 128))


def panel_factor(block):
    columns = [spread(block[:, i : i + 1], 8) for i in range(8)]
    left = {(i, j): spread(columns[j][i : i + 1, :], 8) for i in range(8) for j in range(i, 8)}
    lower, inverse = {}, {}
    for i in range(8):
        scale = lax.rsqrt(left[i, i])
        for j in range(i + 1, 8):
            lower[j, i] = left[i, j] * scale
        for j in range(i + 1, 8):
            for k in range(j, 8):
                left[j, k] = left[j, k] - lower[j, i] * lower[k, i]
        inverse[i, i] = scale
        for j in range(i):
            terms = [lower[i, k] * inverse[k, j] for k in range(j, i)]
            inverse[i, j] = -functools.reduce(jnp.add, terms) * scale
    row = lax.broadcasted_iota(jnp.int32, (8, 128), 0)
    made = []
    for j in range(8):
        column = jnp.zeros((8, 128), f32)
        for i in range(j, 8):
            column = jnp.where(row == i, inverse[i, j], column)
        made.append(column)
    return made


def thirds(a):
    high = a.astype(bf16).astype(f32)
    middle = (a - high).astype(bf16).astype(f32)
    return high, middle, a - high - middle


def begin_inverse(core, a_ref, t_ref):
    rows = lax.broadcasted_iota(jnp.int32, core.shape, 0)
    cols = lax.broadcasted_iota(jnp.int32, core.shape, 1)
    a_ref[...] = core
    t_ref[...] = (rows == cols).astype(f32)


def run_inverse(a_ref, t_ref, start, stop):
    size = a_ref.shape[0]
    rows = lax.broadcasted_iota(jnp.int32, (size, size), 0)

    def step(b, carry):
        first = pl.multiple_of(b * 8, 8)
        line, made = a_ref[pl.ds(first, 8), :], t_ref[pl.ds(first, 8), :]
        factors = panel_factor(pltpu.roll(line, lax.rem(size - first, size), 1))
        line = functools.reduce(jnp.add, [f * spread(line[i : i + 1, :], 8) for i, f in enumerate(factors)])
        made = functools.reduce(jnp.add, [f * spread(made[i : i + 1, :], 8) for i, f in enumerate(factors)])
        t_ref[pl.ds(first, 8), :] = made
        high, middle, low = thirds(jnp.concatenate([line, made], axis=1))
        right = jnp.concatenate([high, middle, high, middle, low, high], axis=0)
        left = jnp.concatenate([high, high, middle, middle, high, low], axis=0)[:, :size]
        change = mm(left.astype(bf16), right.astype(bf16), TN)
        a_ref[...] = a_ref[...] - change[:, :size]
        t_ref[...] = t_ref[...] - jnp.where(rows >= first + 8, change[:, size:], 0.0)
        return carry

    lax.fori_loop(start, stop, step, 0)


def pivot_terms(q_ref, p_ref, core_ref):
    q = q_ref[...]
    pp = p_ref[...]
    width = pp.shape[1] // 2
    p = jnp.concatenate([pp[:, :width], pp[:, width:]], axis=0)
    norm = jnp.sum(p * p, axis=1, keepdims=True)
    across = exact(jnp.ones((8, width), f32), p * p, NT)[:1]
    core_ref[0] = jnp.exp((2.0 * exact(p, p, NT) - norm - across) * (1.0 / width))
    core_ref[1] = exact(q, q, NT)


def shifted(k, g):
    rows = lax.broadcasted_iota(jnp.int32, g.shape, 0)
    cols = lax.broadcasted_iota(jnp.int32, g.shape, 1)
    shift = NUGGET + jnp.max(jnp.sum(jnp.abs(g), axis=1, keepdims=True), axis=0, keepdims=True)
    return k - g + shift * (rows == cols).astype(f32)


def load_rows(place, pivots, turned, points, factor, mine, loads):
    count, width = points.shape
    first = place.number * count
    loads[0].wait()

    def turn(i, carry):
        at = pl.multiple_of(i * 128, 128)
        points[pl.ds(at, 128), :] = turned[:, pl.ds(at, 128)].T
        return carry

    lax.fori_loop(0, count // 128, turn, 0)
    loads[1].wait()
    loads[2].wait()

    def pick(i, carry):
        rows = []
        for s in range(2):
            local = pivots[s, i] - first
            inside = ((local >= 0) & (local < count)).astype(jnp.int32).astype(f32)
            local = jnp.clip(local, 0, count - 1)
            rows.append((points[pl.ds(local, 1), :] * inside, factor[pl.ds(local, 1), :] * inside))
        half, chip = i // CHIPS, i % CHIPS
        for s in range(2):
            for j in range(4):
                mine[half, chip, pl.ds(4 * s + j, 1), :] = rows[s][1][:, 128 * j : 128 * (j + 1)]
        mine[half, chip, pl.ds(8, 1), :] = jnp.concatenate([rows[0][0], rows[1][0]], axis=1)
        return carry

    lax.fori_loop(0, 2 * CHIPS, pick, 0, unroll=4)


def residual(turned, factor, q_ref, p_ref, r_ref, m_ref, qh, ql, pt, pn, flipped, cross, xa, ra, xb, rb):
    width, count = turned.shape
    tile, wide = xa.shape[1:]
    qh[...], ql[...] = halves(q_ref[...].T)
    pp = p_ref[...].T
    p = jnp.concatenate([pp[:width], pp[width:]], axis=1) * (2.0 / width)
    high, low = halves(p)
    pt[...] = jnp.concatenate([high, low, high, low], axis=0)
    pn[...] = jnp.sum(p * p, axis=0, keepdims=True) * (width / 4.0)
    for ref in (flipped, cross, xb, rb):
        ref[...] = jnp.zeros_like(ref)

    def make(first, x, r):
        first = pl.multiple_of(first, tile)
        a = turned[:, pl.ds(first, tile)]
        high, low = halves(a)
        inner = mm(jnp.concatenate([high, high, low, low], axis=0), pt[...], TN)
        norm = jnp.sum(a * a, axis=0, keepdims=True) * (1.0 / width)
        norm = jnp.broadcast_to(norm, (8, tile)).T[:, :1]
        xh, xl = halves(factor[pl.ds(first, tile), :])
        value = jnp.exp(inner - norm - pn[...]) - (mm(xh, qh[...]) + mm(xh, ql[...]) + mm(xl, qh[...]))
        r_ref[pl.ds(first, tile), :] = value
        x[0], x[1] = xh, xl
        r[0], r[1] = halves(value)

    def add(x, r):
        rh, rl = r[0], r[1]
        size = rh.shape[1]
        both = mm(jnp.concatenate([x[0], x[1], rh, rl], axis=1), rh, TN)
        flipped[:wide, :] += both[:wide] + both[wide : 2 * wide] + mm(x[0], rl, TN)
        flipped[wide:, :] += both[2 * wide : 2 * wide + size]
        cross[...] += both[2 * wide + size :]

    def step(i, carry):
        add(xb, rb)
        make(2 * i * tile, xa, ra)
        add(xa, ra)
        make((2 * i + 1) * tile, xb, rb)
        return carry

    lax.fori_loop(0, count // (2 * tile), step, 0)
    add(xb, rb)
    m_ref[:, :wide] = flipped[:wide, :].T
    m_ref[:, wide:] = flipped[wide:, :] + cross[...] + cross[...].T


def main_kernel(pivots_hbm, points_hbm, factor_hbm, r_ref, m_ref, w_ref, pivots, turned, points, factor, load, *rest):
    place = Place()
    loads = [
        pltpu.make_async_copy(points_hbm, turned, load.at[0]),
        pltpu.make_async_copy(pivots_hbm, pivots, load.at[1]),
        pltpu.make_async_copy(factor_hbm, factor, load.at[2]),
    ]
    for copy in loads:
        copy.start()
    greet(place)
    rest = list(rest)
    sum_a, sum_b, rest = rest[:7], rest[7:14], rest[14:]
    q_ref, p_ref, core_ref, a_ref, t_ref, c_ref, *rest = rest
    load_rows(place, pivots, turned, points, factor, sum_a[0], loads)
    greeted()
    device_sum(place, *sum_a)
    total = sum_a[4]
    for half in range(2):
        for s in range(2):
            for j in range(4):
                q_ref[pl.ds(128 * s + CHIPS * half, CHIPS), pl.ds(128 * j, 128)] = total[half, :, 4 * s + j, :]
        p_ref[pl.ds(CHIPS * half, CHIPS), :] = total[half, :, 8, :]

    residual(turned, factor, q_ref, p_ref, r_ref, m_ref, *rest)
    for k in range(2):
        for h in range(2):
            for j in range(6):
                sum_b[0][k, :, 2 * j + h, :] = m_ref[pl.ds(128 * k + CHIPS * h, CHIPS), pl.ds(128 * j, 128)]
    size = a_ref.shape[0]

    def during_swap():
        pivot_terms(q_ref, p_ref, core_ref)
        begin_inverse(shifted(core_ref[0, :size, :size], core_ref[1, :size, :size]), a_ref, t_ref)

    def during_scatter():
        run_inverse(a_ref, t_ref, 0, 12)

    def during_gather():
        run_inverse(a_ref, t_ref, 12, 16)
        turned = t_ref[...].T
        w_ref[:size, :size] = turned
        w_ref[size:, :size] = jnp.zeros((size, size), f32)
        c10 = exact(core_ref[0, size:, :size] - core_ref[1, size:, :size], turned)
        c_ref[...] = c10
        g1 = core_ref[1, size:, size:] + exact(c10, c10, NT)
        begin_inverse(shifted(core_ref[0, size:, size:], g1), a_ref, t_ref)
        run_inverse(a_ref, t_ref, 0, 8)

    def on_the_way_back():
        run_inverse(a_ref, t_ref, 8, 16)
        t1 = t_ref[...]
        w_ref[size:, size:] = t1.T
        w_ref[:size, size:] = -exact(w_ref[:size, :size], exact(t1, c_ref[...]), NT)

    device_sum(place, *sum_b, [during_swap, during_scatter, during_gather, on_the_way_back])
    total = sum_b[4]
    for k in range(2):
        for h in range(2):
            for j in range(6):
                m_ref[pl.ds(128 * k + CHIPS * h, CHIPS), pl.ds(128 * j, 128)] = total[k, :, 2 * j + h, :]


def main(points, factor, pivots, tile=512):
    width, count = points.shape
    wide = factor.shape[1]
    blocks, half = pivots.shape
    size = blocks * half
    return pl.pallas_call(
        main_kernel,
        out_shape=(
            jax.ShapeDtypeStruct((count, size), f32),
            jax.ShapeDtypeStruct((size, wide + size), f32),
            jax.ShapeDtypeStruct((size, size), f32),
        ),
        in_specs=[pl.BlockSpec(memory_space=pltpu.HBM)] * 3,
        out_specs=(pl.BlockSpec(memory_space=pltpu.VMEM),) * 3,
        scratch_shapes=[
            pltpu.SMEM(pivots.shape, jnp.int32),
            pltpu.VMEM((width, count), f32),
            pltpu.VMEM((count, width), f32),
            pltpu.VMEM(factor.shape, f32),
            pltpu.SemaphoreType.DMA((3,)),
            *sum_scratch(9),
            *sum_scratch(12),
            pltpu.VMEM((size, wide), f32),
            pltpu.VMEM((half, 2 * width), f32),
            pltpu.VMEM((2, size, size), f32),
            *[pltpu.VMEM((half, half), f32)] * 3,
            pltpu.VMEM((wide, size), bf16),
            pltpu.VMEM((wide, size), bf16),
            pltpu.VMEM((4 * width, size), bf16),
            pltpu.VMEM((1, size), f32),
            pltpu.VMEM((wide + size, size), f32),
            pltpu.VMEM((size, size), f32),
            *[pltpu.VMEM((2, tile, wide), bf16), pltpu.VMEM((2, tile, size), bf16)] * 2,
        ],
        compiler_params=pltpu.CompilerParams(collective_id=0, has_side_effects=True, vmem_limit_bytes=44 * MB),
    )(pivots, points, factor)


def product(a, b):
    ah, al = halves(a)
    bh, bl = halves(b)
    both = mm(jnp.concatenate([ah, al], axis=0), bh)
    return both[: len(a)] + both[len(a) :] + mm(ah, bl)


def columns_kernel(r_ref, w_ref, m_ref, c_ref, g_ref, *, scale):
    w = w_ref[...]
    c_ref[...] = product(r_ref[...], w)

    @pl.when(pl.program_id(0) == pl.num_programs(0) - 1)
    def _():
        size = w.shape[0]
        wide = m_ref.shape[1] - size
        turned = w.T
        g_ref[:, :wide] = exact(turned, m_ref[:, :wide]) * scale
        g_ref[:, wide:] = exact(turned, exact(m_ref[:, wide:], w)) * scale


def columns(r, w, m, tile=1024):
    count, size = r.shape
    return pl.pallas_call(
        functools.partial(columns_kernel, scale=1.0 / count),
        out_shape=(jax.ShapeDtypeStruct(r.shape, f32), jax.ShapeDtypeStruct(m.shape, f32)),
        grid=(count // tile,),
        in_specs=[
            pl.BlockSpec((tile, size), lambda i: (i, 0)),
            pl.BlockSpec(w.shape, lambda i: (0, 0)),
            pl.BlockSpec(m.shape, lambda i: (0, 0)),
        ],
        out_specs=(pl.BlockSpec((tile, size), lambda i: (i, 0)), pl.BlockSpec(m.shape, lambda i: (0, 0))),
        compiler_params=pltpu.CompilerParams(vmem_limit_bytes=40 * MB),
    )(r, w, m)


def body(points, factor, pivots):
    points = points.T
    r, m, w = main(points, factor, pivots)
    return columns(r, w, m)


def solution(mesh):
    split = P(("row", "col"), None)
    return jax.shard_map(
        body,
        mesh=mesh,
        in_specs=(split, split, P()),
        out_specs=(split, P()),
        check_vma=False,
    )
```

```python
import functools

import jax
import jax.numpy as jnp
from jax import lax
from jax.experimental import pallas as pl
from jax.experimental.pallas import tpu as pltpu
from jax.sharding import PartitionSpec as P

f32 = jnp.float32
bf16 = jnp.bfloat16
MESH = pl.DeviceIdType.MESH
CHIPS = 64
NUGGET = 0.1
MB = 1 << 20

NT = (((1,), (1,)), ((), ()))
TN = (((0,), (0,)), ((), ()))
NN = (((1,), (0,)), ((), ()))


def exact(a, b, dims=NN):
    return lax.dot_general(a, b, dims, precision=lax.Precision.HIGHEST, preferred_element_type=f32)


def mm(a, b, dims=NN):
    return lax.dot_general(a, b, dims, preferred_element_type=f32)


def halves(a):
    high = a.astype(bf16)
    return high, (a - high.astype(f32)).astype(bf16)


PLANES = (2, 1, 3, 0)


def offsets(plane):
    def hops(d):
        return sum(min(c, 4 - c) for c in (d // 4, d % 4))

    return sorted(range(0 if plane else 1, 16), key=lambda d: (-hops(d), d))


class Place:
    def __init__(self):
        row, col = lax.axis_index("row"), lax.axis_index("col")
        self.core, z = row % 2, row // 2
        y, x = col // 4, col % 4
        self.chip = z * 16 + col
        self.number = row * 16 + col
        self.other = (row + 1 - 2 * self.core, col)
        zs = [(z + i) % 4 for i in range(4)]
        ys = [(y + i) % 4 for i in range(4)]
        xs = [(x + i) % 4 for i in range(4)]
        self.ahead = [pl.multiple_of(z * 16, 16) for z in zs]
        self.peers = {}
        for plane in PLANES:
            made = []
            for d in offsets(plane):
                at = ys[d // 4] * 4 + xs[d % 4]
                made.append(((zs[plane] * 2 + self.core, at), zs[plane] * 16 + at))
            self.peers[plane] = made


def greet(place):
    barrier = pltpu.get_barrier_semaphore()
    for plane in PLANES:
        for device, _ in place.peers[plane]:
            pl.semaphore_signal(barrier, inc=1, device_id=device, device_id_type=MESH)
    pl.semaphore_signal(barrier, inc=1, device_id=place.other, device_id_type=MESH)


def greeted():
    pl.semaphore_wait(pltpu.get_barrier_semaphore(), CHIPS)


def remote(src, dst, send, recv, device):
    return pltpu.make_async_remote_copy(src, dst, send, recv, device_id=device, device_id_type=MESH)


def device_sum(place, mine, pair, arrived, own, total, send, recv, work=None):
    core, chip, other = place.core, place.chip, place.other
    work = work or [lambda: None] * 4
    swaps = {}
    for plane in PLANES:
        at = pl.ds(place.ahead[plane], 16)
        swaps[plane] = remote(mine.at[1 - core, at], pair.at[at], send.at[plane], recv.at[plane], other)
        swaps[plane].start()
    work[0]()
    slot = 0
    for plane in PLANES:
        at = pl.ds(place.ahead[plane], 16)
        swaps[plane].wait_recv()
        pair[at] = mine[core, at] + pair[at]
        for device, target in place.peers[plane]:
            remote(pair.at[target], arrived.at[slot], send.at[4], recv.at[4], device).start()
            slot += 1
    work[1]()
    remote(arrived, arrived, send.at[4], recv.at[4], other).wait_recv()
    own[...] = pair[chip] + jnp.sum(arrived[...], axis=0)
    for plane in PLANES:
        for device, _ in place.peers[plane]:
            remote(own, total.at[core, chip], send.at[5 + plane], recv.at[5 + plane], device).start()
    total[core, chip] = own[...]
    work[2]()
    backs = []
    for plane in reversed(PLANES):
        some = arrived.at[pl.ds(0, 16 if plane else 15)]
        remote(some, some, send.at[5 + plane], recv.at[5 + plane], other).wait_recv()
        block = total.at[core, pl.ds(place.ahead[-plane % 4], 16)]
        backs.append(remote(block, block, send.at[9 + plane], recv.at[9 + plane], other))
        backs[-1].start()
    work[3]()
    for plane in PLANES:
        swaps[plane].wait_send()
    remote(arrived, arrived, send.at[4], recv.at[4], other).wait_send()
    for plane in PLANES:
        some = arrived.at[pl.ds(0, 16 if plane else 15)]
        remote(some, some, send.at[5 + plane], recv.at[5 + plane], other).wait_send()
    for back in backs:
        back.wait()


def sum_scratch(rows):
    return [
        pltpu.VMEM((2, CHIPS, rows, 128), f32),
        pltpu.VMEM((CHIPS, rows, 128), f32),
        pltpu.VMEM((CHIPS - 1, rows, 128), f32),
        pltpu.VMEM((rows, 128), f32),
        pltpu.VMEM((2, CHIPS, rows, 128), f32),
        pltpu.SemaphoreType.DMA((13,)),
        pltpu.SemaphoreType.DMA((13,)),
    ]


def spread(a, rows):
    return jnp.broadcast_to(a, (rows, 128))


def panel_factor(block):
    columns = [spread(block[:, i : i + 1], 8) for i in range(8)]
    left = {(i, j): spread(columns[j][i : i + 1, :], 8) for i in range(8) for j in range(i, 8)}
    lower, inverse = {}, {}
    for i in range(8):
        scale = lax.rsqrt(left[i, i])
        for j in range(i + 1, 8):
            lower[j, i] = left[i, j] * scale
        for j in range(i + 1, 8):
            for k in range(j, 8):
                left[j, k] = left[j, k] - lower[j, i] * lower[k, i]
        inverse[i, i] = scale
        for j in range(i):
            terms = [lower[i, k] * inverse[k, j] for k in range(j, i)]
            inverse[i, j] = -functools.reduce(jnp.add, terms) * scale
    row = lax.broadcasted_iota(jnp.int32, (8, 128), 0)
    made = []
    for j in range(8):
        column = jnp.zeros((8, 128), f32)
        for i in range(j, 8):
            column = jnp.where(row == i, inverse[i, j], column)
        made.append(column)
    return made, inverse


def thirds(a):
    high = a.astype(bf16).astype(f32)
    middle = (a - high).astype(bf16).astype(f32)
    return high, middle, a - high - middle


def weighed(factors, rows):
    return functools.reduce(jnp.add, [f * spread(rows[i : i + 1, :], 8) for i, f in enumerate(factors)])


def begin_inverse(core, state):
    a_ref, t_ref, panel_ref, left_ref, right_ref = state
    rows = lax.broadcasted_iota(jnp.int32, core.shape, 0)
    cols = lax.broadcasted_iota(jnp.int32, core.shape, 1)
    a_ref[...] = core
    t_ref[...] = (rows == cols).astype(f32)
    panel_ref[0], panel_ref[1] = a_ref[:8, :], t_ref[:8, :]
    left_ref[...] = jnp.zeros_like(left_ref)
    right_ref[...] = jnp.zeros_like(right_ref)


def run_inverse(state, start, stop):
    a_ref, t_ref, panel_ref, left_ref, right_ref = state
    size = a_ref.shape[0]
    rows = lax.broadcasted_iota(jnp.int32, (size, size), 0)

    def step(b, carry):
        first = pl.multiple_of(b * 8, 8)
        after = pl.multiple_of(lax.rem(first + 8, size), 8)
        turn = lax.rem(size - first, size)
        line, made = panel_ref[0], panel_ref[1]
        change = mm(left_ref[...], right_ref[...], TN)
        a_ref[...] = a_ref[...] - change[:, :size]
        t_ref[...] = t_ref[...] - jnp.where(rows >= first, change[:, size:], 0.0)
        factors, inverse = panel_factor(pltpu.roll(line, turn, 1))
        line, made = weighed(factors, line), weighed(factors, made)
        later, built = a_ref[pl.ds(after, 8), :], t_ref[pl.ds(after, 8), :]
        t_ref[pl.ds(first, 8), :] = made
        block = pltpu.roll(later, turn, 1)
        columns = [spread(block[:, i : i + 1], 8) for i in range(8)]
        scales = [functools.reduce(jnp.add, [inverse[i, j] * columns[j] for j in range(i + 1)]) for i in range(8)]
        panel_ref[0] = later - weighed(scales, line)
        panel_ref[1] = built - weighed(scales, made)
        high, middle, low = thirds(jnp.concatenate([line, made], axis=1))
        right_ref[...] = jnp.concatenate([high, middle, high, middle, low, high], axis=0).astype(bf16)
        left_ref[...] = jnp.concatenate([high, high, middle, middle, high, low], axis=0)[:, :size].astype(bf16)
        return carry

    lax.fori_loop(start, stop, step, 0)


def pivot_terms(q_ref, p_ref, core_ref):
    q = q_ref[...]
    pp = p_ref[...]
    width = pp.shape[1] // 2
    p = jnp.concatenate([pp[:, :width], pp[:, width:]], axis=0)
    norm = jnp.sum(p * p, axis=1, keepdims=True)
    across = exact(jnp.ones((8, width), f32), p * p, NT)[:1]
    core_ref[0] = jnp.exp((2.0 * exact(p, p, NT) - norm - across) * (1.0 / width))
    core_ref[1] = exact(q, q, NT)


def shifted(k, g):
    rows = lax.broadcasted_iota(jnp.int32, g.shape, 0)
    cols = lax.broadcasted_iota(jnp.int32, g.shape, 1)
    shift = NUGGET + jnp.max(jnp.sum(jnp.abs(g), axis=1, keepdims=True), axis=0, keepdims=True)
    return k - g + shift * (rows == cols).astype(f32)


def load_rows(place, pivots, turned, points, factor, mine, loads):
    count, width = points.shape
    first = place.number * count
    loads[0].wait()

    def turn(i, carry):
        at = pl.multiple_of(i * 128, 128)
        points[pl.ds(at, 128), :] = turned[:, pl.ds(at, 128)].T
        return carry

    lax.fori_loop(0, count // 128, turn, 0)
    loads[1].wait()
    loads[2].wait()

    def pick(i, carry):
        rows = []
        for s in range(2):
            local = pivots[s, i] - first
            inside = ((local >= 0) & (local < count)).astype(jnp.int32).astype(f32)
            local = jnp.clip(local, 0, count - 1)
            rows.append((points[pl.ds(local, 1), :] * inside, factor[pl.ds(local, 1), :] * inside))
        half, chip = i // CHIPS, i % CHIPS
        for s in range(2):
            for j in range(4):
                mine[half, chip, pl.ds(4 * s + j, 1), :] = rows[s][1][:, 128 * j : 128 * (j + 1)]
        mine[half, chip, pl.ds(8, 1), :] = jnp.concatenate([rows[0][0], rows[1][0]], axis=1)
        return carry

    lax.fori_loop(0, 2 * CHIPS, pick, 0, unroll=4)


def residual(turned, factor, q_ref, p_ref, r_ref, m_ref, qh, ql, pt, pn, flipped, cross, xa, ra, xb, rb):
    width, count = turned.shape
    tile, wide = xa.shape[1:]
    qh[...], ql[...] = halves(q_ref[...].T)
    pp = p_ref[...].T
    p = jnp.concatenate([pp[:width], pp[width:]], axis=1) * (2.0 / width)
    high, low = halves(p)
    pt[...] = jnp.concatenate([high, low, high, low], axis=0)
    pn[...] = jnp.sum(p * p, axis=0, keepdims=True) * (width / 4.0)
    for ref in (flipped, cross, xb, rb):
        ref[...] = jnp.zeros_like(ref)

    def make(first, x, r):
        first = pl.multiple_of(first, tile)
        a = turned[:, pl.ds(first, tile)]
        high, low = halves(a)
        inner = mm(jnp.concatenate([high, high, low, low], axis=0), pt[...], TN)
        norm = jnp.sum(a * a, axis=0, keepdims=True) * (1.0 / width)
        norm = jnp.broadcast_to(norm, (8, tile)).T[:, :1]
        xh, xl = halves(factor[pl.ds(first, tile), :])
        value = jnp.exp(inner - norm - pn[...]) - (mm(xh, qh[...]) + mm(xh, ql[...]) + mm(xl, qh[...]))
        r_ref[pl.ds(first, tile), :] = value
        x[0], x[1] = xh, xl
        r[0], r[1] = halves(value)

    def add(x, r):
        rh, rl = r[0], r[1]
        size = rh.shape[1]
        both = mm(jnp.concatenate([x[0], x[1], rh, rl], axis=1), rh, TN)
        flipped[:wide, :] += both[:wide] + both[wide : 2 * wide] + mm(x[0], rl, TN)
        flipped[wide:, :] += both[2 * wide : 2 * wide + size]
        cross[...] += both[2 * wide + size :]

    def step(i, carry):
        add(xb, rb)
        make(2 * i * tile, xa, ra)
        add(xa, ra)
        make((2 * i + 1) * tile, xb, rb)
        return carry

    lax.fori_loop(0, count // (2 * tile), step, 0)
    add(xb, rb)
    m_ref[:, :wide] = flipped[:wide, :].T
    m_ref[:, wide:] = flipped[wide:, :] + cross[...] + cross[...].T


def main_kernel(pivots_hbm, points_hbm, factor_hbm, r_ref, m_ref, w_ref, pivots, turned, points, factor, load, *rest):
    place = Place()
    loads = [
        pltpu.make_async_copy(points_hbm, turned, load.at[0]),
        pltpu.make_async_copy(pivots_hbm, pivots, load.at[1]),
        pltpu.make_async_copy(factor_hbm, factor, load.at[2]),
    ]
    for copy in loads:
        copy.start()
    greet(place)
    rest = list(rest)
    sum_a, sum_b, rest = rest[:7], rest[7:14], rest[14:]
    q_ref, p_ref, core_ref, c_ref, *rest = rest
    state, rest = rest[:5], rest[5:]
    t_ref = state[1]
    load_rows(place, pivots, turned, points, factor, sum_a[0], loads)
    greeted()
    device_sum(place, *sum_a)
    total = sum_a[4]
    for half in range(2):
        for s in range(2):
            for j in range(4):
                q_ref[pl.ds(128 * s + CHIPS * half, CHIPS), pl.ds(128 * j, 128)] = total[half, :, 4 * s + j, :]
        p_ref[pl.ds(CHIPS * half, CHIPS), :] = total[half, :, 8, :]

    residual(turned, factor, q_ref, p_ref, r_ref, m_ref, *rest)
    for k in range(2):
        for h in range(2):
            for j in range(6):
                sum_b[0][k, :, 2 * j + h, :] = m_ref[pl.ds(128 * k + CHIPS * h, CHIPS), pl.ds(128 * j, 128)]
    size = t_ref.shape[0]

    def during_swap():
        pivot_terms(q_ref, p_ref, core_ref)
        begin_inverse(shifted(core_ref[0, :size, :size], core_ref[1, :size, :size]), state)

    def during_scatter():
        run_inverse(state, 0, 16)

    def during_gather():
        turned = t_ref[...].T
        w_ref[:size, :size] = turned
        w_ref[size:, :size] = jnp.zeros((size, size), f32)
        c10 = exact(core_ref[0, size:, :size] - core_ref[1, size:, :size], turned)
        c_ref[...] = c10
        g1 = core_ref[1, size:, size:] + exact(c10, c10, NT)
        begin_inverse(shifted(core_ref[0, size:, size:], g1), state)
        run_inverse(state, 0, 12)

    def on_the_way_back():
        run_inverse(state, 12, 16)
        t1 = t_ref[...]
        w_ref[size:, size:] = t1.T
        w_ref[:size, size:] = -exact(w_ref[:size, :size], exact(t1, c_ref[...]), NT)

    device_sum(place, *sum_b, [during_swap, during_scatter, during_gather, on_the_way_back])
    total = sum_b[4]
    for k in range(2):
        for h in range(2):
            for j in range(6):
                m_ref[pl.ds(128 * k + CHIPS * h, CHIPS), pl.ds(128 * j, 128)] = total[k, :, 2 * j + h, :]


def main(points, factor, pivots, tile=512):
    width, count = points.shape
    wide = factor.shape[1]
    blocks, half = pivots.shape
    size = blocks * half
    return pl.pallas_call(
        main_kernel,
        out_shape=(
            jax.ShapeDtypeStruct((count, size), f32),
            jax.ShapeDtypeStruct((size, wide + size), f32),
            jax.ShapeDtypeStruct((size, size), f32),
        ),
        in_specs=[pl.BlockSpec(memory_space=pltpu.HBM)] * 3,
        out_specs=(pl.BlockSpec(memory_space=pltpu.VMEM),) * 3,
        scratch_shapes=[
            pltpu.SMEM(pivots.shape, jnp.int32),
            pltpu.VMEM((width, count), f32),
            pltpu.VMEM((count, width), f32),
            pltpu.VMEM(factor.shape, f32),
            pltpu.SemaphoreType.DMA((3,)),
            *sum_scratch(9),
            *sum_scratch(12),
            pltpu.VMEM((size, wide), f32),
            pltpu.VMEM((half, 2 * width), f32),
            pltpu.VMEM((2, size, size), f32),
            *[pltpu.VMEM((half, half), f32)] * 3,
            pltpu.VMEM((2, 8, half), f32),
            pltpu.VMEM((48, half), bf16),
            pltpu.VMEM((48, 2 * half), bf16),
            pltpu.VMEM((wide, size), bf16),
            pltpu.VMEM((wide, size), bf16),
            pltpu.VMEM((4 * width, size), bf16),
            pltpu.VMEM((1, size), f32),
            pltpu.VMEM((wide + size, size), f32),
            pltpu.VMEM((size, size), f32),
            *[pltpu.VMEM((2, tile, wide), bf16), pltpu.VMEM((2, tile, size), bf16)] * 2,
        ],
        compiler_params=pltpu.CompilerParams(collective_id=0, has_side_effects=True, vmem_limit_bytes=44 * MB),
    )(pivots, points, factor)


def product(a, b):
    ah, al = halves(a)
    bh, bl = halves(b)
    both = mm(jnp.concatenate([ah, al], axis=0), bh)
    return both[: len(a)] + both[len(a) :] + mm(ah, bl)


def columns_kernel(r_ref, w_ref, m_ref, c_ref, g_ref, *, scale):
    w = w_ref[...]
    c_ref[...] = product(r_ref[...], w)

    @pl.when(pl.program_id(0) == pl.num_programs(0) - 1)
    def _():
        size = w.shape[0]
        wide = m_ref.shape[1] - size
        turned = w.T
        g_ref[:, :wide] = exact(turned, m_ref[:, :wide]) * scale
        g_ref[:, wide:] = exact(turned, exact(m_ref[:, wide:], w)) * scale


def columns(r, w, m, tile=1024):
    count, size = r.shape
    return pl.pallas_call(
        functools.partial(columns_kernel, scale=1.0 / count),
        out_shape=(jax.ShapeDtypeStruct(r.shape, f32), jax.ShapeDtypeStruct(m.shape, f32)),
        grid=(count // tile,),
        in_specs=[
            pl.BlockSpec((tile, size), lambda i: (i, 0)),
            pl.BlockSpec(w.shape, lambda i: (0, 0)),
            pl.BlockSpec(m.shape, lambda i: (0, 0)),
        ],
        out_specs=(pl.BlockSpec((tile, size), lambda i: (i, 0)), pl.BlockSpec(m.shape, lambda i: (0, 0))),
        compiler_params=pltpu.CompilerParams(vmem_limit_bytes=40 * MB),
    )(r, w, m)


def body(points, factor, pivots):
    points = points.T
    r, m, w = main(points, factor, pivots)
    return columns(r, w, m)


def solution(mesh):
    split = P(("row", "col"), None)
    return jax.shard_map(
        body,
        mesh=mesh,
        in_specs=(split, split, P()),
        out_specs=(split, P()),
        check_vma=False,
    )
```

```python
import functools

import jax
import jax.numpy as jnp
from jax import lax
from jax.experimental import pallas as pl
from jax.experimental.pallas import tpu as pltpu
from jax.sharding import PartitionSpec as P

f32 = jnp.float32
bf16 = jnp.bfloat16
MESH = pl.DeviceIdType.MESH
CHIPS = 64
NUGGET = 0.1
MB = 1 << 20

NT = (((1,), (1,)), ((), ()))
TN = (((0,), (0,)), ((), ()))
NN = (((1,), (0,)), ((), ()))


def exact(a, b, dims=NN):
    return lax.dot_general(a, b, dims, precision=lax.Precision.HIGHEST, preferred_element_type=f32)


def mm(a, b, dims=NN):
    return lax.dot_general(a, b, dims, preferred_element_type=f32)


def halves(a):
    high = a.astype(bf16)
    return high, (a - high.astype(f32)).astype(bf16)


PLANES = (2, 1, 3, 0)


def offsets(plane):
    def hops(d):
        return sum(min(c, 4 - c) for c in (d // 4, d % 4))

    return sorted(range(0 if plane else 1, 16), key=lambda d: (-hops(d), d))


class Place:
    def __init__(self):
        row, col = lax.axis_index("row"), lax.axis_index("col")
        self.core, z = row % 2, row // 2
        y, x = col // 4, col % 4
        self.chip = z * 16 + col
        self.number = row * 16 + col
        self.other = (row + 1 - 2 * self.core, col)
        zs = [(z + i) % 4 for i in range(4)]
        ys = [(y + i) % 4 for i in range(4)]
        xs = [(x + i) % 4 for i in range(4)]
        self.ahead = [pl.multiple_of(z * 16, 16) for z in zs]
        self.peers = {}
        for plane in PLANES:
            made = []
            for d in offsets(plane):
                at = ys[d // 4] * 4 + xs[d % 4]
                made.append(((zs[plane] * 2 + self.core, at), zs[plane] * 16 + at))
            self.peers[plane] = made


def greet(place):
    barrier = pltpu.get_barrier_semaphore()
    for plane in PLANES:
        for device, _ in place.peers[plane]:
            pl.semaphore_signal(barrier, inc=1, device_id=device, device_id_type=MESH)
    pl.semaphore_signal(barrier, inc=1, device_id=place.other, device_id_type=MESH)


def greeted():
    pl.semaphore_wait(pltpu.get_barrier_semaphore(), CHIPS)


def remote(src, dst, send, recv, device):
    return pltpu.make_async_remote_copy(src, dst, send, recv, device_id=device, device_id_type=MESH)


def device_sum(place, mine, pair, arrived, own, total, send, recv, work=None):
    core, chip, other = place.core, place.chip, place.other
    work = work or [lambda: None] * 4
    swaps = {}
    for plane in PLANES:
        at = pl.ds(place.ahead[plane], 16)
        swaps[plane] = remote(mine.at[1 - core, at], pair.at[at], send.at[plane], recv.at[plane], other)
        swaps[plane].start()
    work[0]()
    slot = 0
    for plane in PLANES:
        at = pl.ds(place.ahead[plane], 16)
        swaps[plane].wait_recv()
        pair[at] = mine[core, at] + pair[at]
        for device, target in place.peers[plane]:
            remote(pair.at[target], arrived.at[slot], send.at[4], recv.at[4], device).start()
            slot += 1
    work[1]()
    remote(arrived, arrived, send.at[4], recv.at[4], other).wait_recv()
    own[...] = pair[chip] + jnp.sum(arrived[...], axis=0)
    for plane in PLANES:
        for device, _ in place.peers[plane]:
            remote(own, total.at[core, chip], send.at[5 + plane], recv.at[5 + plane], device).start()
    total[core, chip] = own[...]
    work[2]()
    backs = []
    for plane in reversed(PLANES):
        some = arrived.at[pl.ds(0, 16 if plane else 15)]
        remote(some, some, send.at[5 + plane], recv.at[5 + plane], other).wait_recv()
        block = total.at[core, pl.ds(place.ahead[-plane % 4], 16)]
        backs.append(remote(block, block, send.at[9 + plane], recv.at[9 + plane], other))
        backs[-1].start()
    work[3]()
    for plane in PLANES:
        swaps[plane].wait_send()
    remote(arrived, arrived, send.at[4], recv.at[4], other).wait_send()
    for plane in PLANES:
        some = arrived.at[pl.ds(0, 16 if plane else 15)]
        remote(some, some, send.at[5 + plane], recv.at[5 + plane], other).wait_send()
    for back in backs:
        back.wait()


def sum_scratch(rows):
    return [
        pltpu.VMEM((2, CHIPS, rows, 128), f32),
        pltpu.VMEM((CHIPS, rows, 128), f32),
        pltpu.VMEM((CHIPS - 1, rows, 128), f32),
        pltpu.VMEM((rows, 128), f32),
        pltpu.VMEM((2, CHIPS, rows, 128), f32),
        pltpu.SemaphoreType.DMA((13,)),
        pltpu.SemaphoreType.DMA((13,)),
    ]


def spread(a, rows):
    return jnp.broadcast_to(a, (rows, 128))


def panel_factor(block):
    columns = [spread(block[:, i : i + 1], 8) for i in range(8)]
    left = {(i, j): spread(columns[j][i : i + 1, :], 8) for i in range(8) for j in range(i, 8)}
    lower, inverse = {}, {}
    for i in range(8):
        scale = lax.rsqrt(left[i, i])
        for j in range(i + 1, 8):
            lower[j, i] = left[i, j] * scale
        for j in range(i + 1, 8):
            for k in range(j, 8):
                left[j, k] = left[j, k] - lower[j, i] * lower[k, i]
        inverse[i, i] = scale
        for j in range(i):
            terms = [lower[i, k] * inverse[k, j] for k in range(j, i)]
            inverse[i, j] = -functools.reduce(jnp.add, terms) * scale
    row = lax.broadcasted_iota(jnp.int32, (8, 128), 0)
    made = []
    for j in range(8):
        column = jnp.zeros((8, 128), f32)
        for i in range(j, 8):
            column = jnp.where(row == i, inverse[i, j], column)
        made.append(column)
    return made, inverse


def thirds(a):
    high = a.astype(bf16).astype(f32)
    middle = (a - high).astype(bf16).astype(f32)
    return high, middle, a - high - middle


def weighed(factors, rows):
    return functools.reduce(jnp.add, [f * spread(rows[i : i + 1, :], 8) for i, f in enumerate(factors)])


def begin_inverse(core, state):
    a_ref, t_ref, panel_ref, left_ref, right_ref = state
    rows = lax.broadcasted_iota(jnp.int32, core.shape, 0)
    cols = lax.broadcasted_iota(jnp.int32, core.shape, 1)
    a_ref[...] = core
    t_ref[...] = (rows == cols).astype(f32)
    panel_ref[0], panel_ref[1] = a_ref[:8, :], t_ref[:8, :]
    left_ref[...] = jnp.zeros_like(left_ref)
    right_ref[...] = jnp.zeros_like(right_ref)


def run_inverse(state, start, stop):
    a_ref, t_ref, panel_ref, left_ref, right_ref = state
    size = a_ref.shape[0]
    rows = lax.broadcasted_iota(jnp.int32, (size, size), 0)

    def step(b, carry):
        first = pl.multiple_of(b * 8, 8)
        after = pl.multiple_of(lax.rem(first + 8, size), 8)
        turn = lax.rem(size - first, size)
        line, made = panel_ref[0], panel_ref[1]
        change = mm(left_ref[...], right_ref[...], TN)
        a_ref[...] = a_ref[...] - change[:, :size]
        t_ref[...] = t_ref[...] - jnp.where(rows >= first, change[:, size:], 0.0)
        factors, inverse = panel_factor(pltpu.roll(line, turn, 1))
        line, made = weighed(factors, line), weighed(factors, made)
        later, built = a_ref[pl.ds(after, 8), :], t_ref[pl.ds(after, 8), :]
        t_ref[pl.ds(first, 8), :] = made
        block = pltpu.roll(later, turn, 1)
        columns = [spread(block[:, i : i + 1], 8) for i in range(8)]
        scales = [functools.reduce(jnp.add, [inverse[i, j] * columns[j] for j in range(i + 1)]) for i in range(8)]
        panel_ref[0] = later - weighed(scales, line)
        panel_ref[1] = built - weighed(scales, made)
        high, middle, low = thirds(jnp.concatenate([line, made], axis=1))
        right_ref[...] = jnp.concatenate([high, middle, high, middle, low, high], axis=0).astype(bf16)
        left_ref[...] = jnp.concatenate([high, high, middle, middle, high, low], axis=0)[:, :size].astype(bf16)
        return carry

    lax.fori_loop(start, stop, step, 0)


def pivot_terms(q_ref, p_ref, core_ref):
    q = q_ref[...]
    pp = p_ref[...]
    width = pp.shape[1] // 2
    p = jnp.concatenate([pp[:, :width], pp[:, width:]], axis=0)
    norm = jnp.sum(p * p, axis=1, keepdims=True)
    across = exact(jnp.ones((8, width), f32), p * p, NT)[:1]
    core_ref[0] = jnp.exp((2.0 * exact(p, p, NT) - norm - across) * (1.0 / width))
    core_ref[1] = exact(q, q, NT)


def shifted(k, g):
    rows = lax.broadcasted_iota(jnp.int32, g.shape, 0)
    cols = lax.broadcasted_iota(jnp.int32, g.shape, 1)
    shift = NUGGET + jnp.max(jnp.sum(jnp.abs(g), axis=1, keepdims=True), axis=0, keepdims=True)
    return k - g + shift * (rows == cols).astype(f32)


def load_rows(place, pivots, turned, points, factor, mine, loads):
    count, width = points.shape
    first = place.number * count
    loads[0].wait()

    def turn(i, carry):
        at = pl.multiple_of(i * 128, 128)
        points[pl.ds(at, 128), :] = turned[:, pl.ds(at, 128)].T
        return carry

    lax.fori_loop(0, count // 128, turn, 0)
    loads[1].wait()
    loads[2].wait()

    def pick(i, carry):
        rows = []
        for s in range(2):
            local = pivots[s, i] - first
            inside = ((local >= 0) & (local < count)).astype(jnp.int32).astype(f32)
            local = jnp.clip(local, 0, count - 1)
            rows.append((points[pl.ds(local, 1), :] * inside, factor[pl.ds(local, 1), :] * inside))
        half, chip = i // CHIPS, i % CHIPS
        for s in range(2):
            for j in range(4):
                mine[half, chip, pl.ds(4 * s + j, 1), :] = rows[s][1][:, 128 * j : 128 * (j + 1)]
        mine[half, chip, pl.ds(8, 1), :] = jnp.concatenate([rows[0][0], rows[1][0]], axis=1)
        return carry

    lax.fori_loop(0, 2 * CHIPS, pick, 0, unroll=4)


def residual(turned, factor, q_ref, p_ref, r_ref, m_ref, qh, ql, pt, pn, flipped, cross, xa, ra, xb, rb):
    width, count = turned.shape
    tile, wide = xa.shape[1:]
    qh[...], ql[...] = halves(q_ref[...].T)
    pp = p_ref[...].T
    p = jnp.concatenate([pp[:width], pp[width:]], axis=1) * (2.0 / width)
    high, low = halves(p)
    pt[...] = jnp.concatenate([high, low, high, low], axis=0)
    pn[...] = jnp.sum(p * p, axis=0, keepdims=True) * (width / 4.0)
    for ref in (flipped, cross, xb, rb):
        ref[...] = jnp.zeros_like(ref)

    def make(first, x, r):
        first = pl.multiple_of(first, tile)
        a = turned[:, pl.ds(first, tile)]
        high, low = halves(a)
        inner = mm(jnp.concatenate([high, high, low, low], axis=0), pt[...], TN)
        norm = jnp.sum(a * a, axis=0, keepdims=True) * (1.0 / width)
        norm = jnp.broadcast_to(norm, (8, tile)).T[:, :1]
        xh, xl = halves(factor[pl.ds(first, tile), :])
        value = jnp.exp(inner - norm - pn[...]) - (mm(xh, qh[...]) + mm(xh, ql[...]) + mm(xl, qh[...]))
        r_ref[pl.ds(first, tile), :] = value
        x[0], x[1] = xh, xl
        r[0], r[1] = halves(value)

    def add(x, r):
        rh, rl = r[0], r[1]
        size = rh.shape[1]
        both = mm(jnp.concatenate([x[0], x[1], rh, rl], axis=1), rh, TN)
        flipped[:wide, :] += both[:wide] + both[wide : 2 * wide] + mm(x[0], rl, TN)
        flipped[wide:, :] += both[2 * wide : 2 * wide + size]
        cross[...] += both[2 * wide + size :]

    def step(i, carry):
        add(xb, rb)
        make(2 * i * tile, xa, ra)
        add(xa, ra)
        make((2 * i + 1) * tile, xb, rb)
        return carry

    lax.fori_loop(0, count // (2 * tile), step, 0)
    add(xb, rb)
    m_ref[:, :wide] = flipped[:wide, :].T
    m_ref[:, wide:] = flipped[wide:, :] + cross[...] + cross[...].T


def main_kernel(pivots_hbm, points_hbm, factor_hbm, r_ref, m_ref, w_ref, pivots, turned, points, factor, load, *rest):
    place = Place()
    loads = [
        pltpu.make_async_copy(points_hbm, turned, load.at[0]),
        pltpu.make_async_copy(pivots_hbm, pivots, load.at[1]),
        pltpu.make_async_copy(factor_hbm, factor, load.at[2]),
    ]
    for copy in loads:
        copy.start()
    greet(place)
    rest = list(rest)
    sum_a, sum_b, rest = rest[:7], rest[7:14], rest[14:]
    q_ref, p_ref, core_ref, c_ref, *rest = rest
    state, rest = rest[:5], rest[5:]
    t_ref = state[1]
    load_rows(place, pivots, turned, points, factor, sum_a[0], loads)
    greeted()
    device_sum(place, *sum_a)
    total = sum_a[4]
    for half in range(2):
        for s in range(2):
            for j in range(4):
                q_ref[pl.ds(128 * s + CHIPS * half, CHIPS), pl.ds(128 * j, 128)] = total[half, :, 4 * s + j, :]
        p_ref[pl.ds(CHIPS * half, CHIPS), :] = total[half, :, 8, :]

    residual(turned, factor, q_ref, p_ref, r_ref, m_ref, *rest)
    for k in range(2):
        for h in range(2):
            for j in range(6):
                sum_b[0][k, :, 2 * j + h, :] = m_ref[pl.ds(128 * k + CHIPS * h, CHIPS), pl.ds(128 * j, 128)]
    size = t_ref.shape[0]

    def during_swap():
        pivot_terms(q_ref, p_ref, core_ref)
        begin_inverse(shifted(core_ref[0, :size, :size], core_ref[1, :size, :size]), state)

    def during_scatter():
        run_inverse(state, 0, 16)

    def during_gather():
        turned = t_ref[...].T
        w_ref[:size, :size] = turned
        w_ref[size:, :size] = jnp.zeros((size, size), f32)
        c10 = exact(core_ref[0, size:, :size] - core_ref[1, size:, :size], turned)
        c_ref[...] = c10
        g1 = core_ref[1, size:, size:] + exact(c10, c10, NT)
        begin_inverse(shifted(core_ref[0, size:, size:], g1), state)
        run_inverse(state, 0, 14)

    def on_the_way_back():
        run_inverse(state, 14, 16)
        t1 = t_ref[...]
        w_ref[size:, size:] = t1.T
        w_ref[:size, size:] = -exact(w_ref[:size, :size], exact(t1, c_ref[...]), NT)

    device_sum(place, *sum_b, [during_swap, during_scatter, during_gather, on_the_way_back])
    total = sum_b[4]
    for k in range(2):
        for h in range(2):
            for j in range(6):
                m_ref[pl.ds(128 * k + CHIPS * h, CHIPS), pl.ds(128 * j, 128)] = total[k, :, 2 * j + h, :]


def main(points, factor, pivots, tile=512):
    width, count = points.shape
    wide = factor.shape[1]
    blocks, half = pivots.shape
    size = blocks * half
    return pl.pallas_call(
        main_kernel,
        out_shape=(
            jax.ShapeDtypeStruct((count, size), f32),
            jax.ShapeDtypeStruct((size, wide + size), f32),
            jax.ShapeDtypeStruct((size, size), f32),
        ),
        in_specs=[pl.BlockSpec(memory_space=pltpu.HBM)] * 3,
        out_specs=(pl.BlockSpec(memory_space=pltpu.VMEM),) * 3,
        scratch_shapes=[
            pltpu.SMEM(pivots.shape, jnp.int32),
            pltpu.VMEM((width, count), f32),
            pltpu.VMEM((count, width), f32),
            pltpu.VMEM(factor.shape, f32),
            pltpu.SemaphoreType.DMA((3,)),
            *sum_scratch(9),
            *sum_scratch(12),
            pltpu.VMEM((size, wide), f32),
            pltpu.VMEM((half, 2 * width), f32),
            pltpu.VMEM((2, size, size), f32),
            *[pltpu.VMEM((half, half), f32)] * 3,
            pltpu.VMEM((2, 8, half), f32),
            pltpu.VMEM((48, half), bf16),
            pltpu.VMEM((48, 2 * half), bf16),
            pltpu.VMEM((wide, size), bf16),
            pltpu.VMEM((wide, size), bf16),
            pltpu.VMEM((4 * width, size), bf16),
            pltpu.VMEM((1, size), f32),
            pltpu.VMEM((wide + size, size), f32),
            pltpu.VMEM((size, size), f32),
            *[pltpu.VMEM((2, tile, wide), bf16), pltpu.VMEM((2, tile, size), bf16)] * 2,
        ],
        compiler_params=pltpu.CompilerParams(collective_id=0, has_side_effects=True, vmem_limit_bytes=44 * MB),
    )(pivots, points, factor)


def product(a, b):
    ah, al = halves(a)
    bh, bl = halves(b)
    both = mm(jnp.concatenate([ah, al], axis=0), bh)
    return both[: len(a)] + both[len(a) :] + mm(ah, bl)


def columns_kernel(r_ref, w_ref, m_ref, c_ref, g_ref, *, scale):
    w = w_ref[...]
    c_ref[...] = product(r_ref[...], w)

    @pl.when(pl.program_id(0) == pl.num_programs(0) - 1)
    def _():
        size = w.shape[0]
        wide = m_ref.shape[1] - size
        turned = w.T
        g_ref[:, :wide] = exact(turned, m_ref[:, :wide]) * scale
        g_ref[:, wide:] = exact(turned, exact(m_ref[:, wide:], w)) * scale


def columns(r, w, m, tile=2048):
    count, size = r.shape
    return pl.pallas_call(
        functools.partial(columns_kernel, scale=1.0 / count),
        out_shape=(jax.ShapeDtypeStruct(r.shape, f32), jax.ShapeDtypeStruct(m.shape, f32)),
        grid=(count // tile,),
        in_specs=[
            pl.BlockSpec((tile, size), lambda i: (i, 0)),
            pl.BlockSpec(w.shape, lambda i: (0, 0)),
            pl.BlockSpec(m.shape, lambda i: (0, 0)),
        ],
        out_specs=(pl.BlockSpec((tile, size), lambda i: (i, 0)), pl.BlockSpec(m.shape, lambda i: (0, 0))),
        compiler_params=pltpu.CompilerParams(vmem_limit_bytes=40 * MB),
    )(r, w, m)


def body(points, factor, pivots):
    points = points.T
    r, m, w = main(points, factor, pivots)
    return columns(r, w, m)


def solution(mesh):
    split = P(("row", "col"), None)
    return jax.shard_map(
        body,
        mesh=mesh,
        in_specs=(split, split, P()),
        out_specs=(split, P()),
        check_vma=False,
    )
```
